32 devices in a mesh: lat: 2 (over y), lon: 16 (over z, x, core).
Axes of the slice: x: 2, y: 2, z: 4, core: 2. Of those that a mesh axis runs over, the one named last changes fastest.
Arguments:
- sea_level: float32 [2048, 256], P('lon', 'lat'), may hold values from -1 to 5
- east_velocity: float32 [2048, 256], P('lon', 'lat'), may hold values from -6 to 6
- north_velocity: float32 [2048, 256], P('lon', 'lat'), may hold values from -6 to 6
- depth: float32 [2048, 256], P('lon', 'lat'), may hold values from 0.25 to 1
- land_mask: int32 [2048, 256], P('lon', 'lat'), may hold values from 0 to 1, as said below
- wet_counts: int32 [2, 16], replicated, may hold values from 1 to 16384, as said below
- loading_prev: float32 [2048, 256], P('lon', 'lat'), may hold values from -4 to 4
- tide_amp: float32 [8], replicated, may hold values from 0.3 to 1
- tide_phase: float32 [8], replicated, may hold values from -3.140625 to 3.140625
- legendre: bfloat16 [512, 1024, 256], P('lon', None, 'lat'), may hold values from -0.375 to 0.375
- love_factor: float32 [1024], replicated, may hold values from 0.05 to 1
Outputs:
- height_new: float32 [2048, 256], P('lon', 'lat')
- east_new: float32 [2048, 256], P('lon', 'lat')
- north_new: float32 [2048, 256], P('lon', 'lat')
- self_attraction: float32 [2048, 256], P('lon', 'lat')
The draws below stay inside these ranges and needn't reach their ends.
Inputs may be any that keep to these rules, and one draw needn't show every extreme that they name: `land_mask`: every tile of 128 columns by 128 rows holds at least one wet column, and one tile is wholly wet. wet_counts[p, q] is the number of wet columns of land_mask in latitude band p and longitude band q.
All inputs are finite; a program needn't handle non-finite values.
Results may differ from the reference program's by a relative error of at most 0.0038.
Values may be sent and summed in bfloat16 or wider, within the bound.
No kernel may reach another device: no remote copies, remote signals or barrier semaphores. Data moves between devices by JAX's collectives and lax.ppermute only.
A program may use at most 64 MiB of HBM per device.

```python
import math
import jax
import jax.numpy as jnp
from jax import lax

LON_DEV = 128
LAT_DEV = 128
NDEG = 1024
SUBSTEPS = 4
CONSTITUENTS = 8
NLON = 2048
NLAT = 256
M = 512
BANDS_LON = 16
BANDS_LAT = 2


def draw_sea_level(key, part):
    rows = lax.broadcasted_iota(jnp.int32, (NLON, NLAT), 1).astype(jnp.float32)
    base = 1.0 + 2.0 * rows / NLAT
    noise = jnp.clip(jax.random.normal(key, (NLON, NLAT), jnp.float32), -4.0, 4.0)
    return base + 0.5 * noise


def wet_table(key):
    values = jax.random.randint(jax.random.fold_in(key, 7), (NLON, NLAT), 0, 5)
    full_lon = jax.random.randint(jax.random.fold_in(key, 11), (), 0, BANDS_LON)
    full_lat = jax.random.randint(jax.random.fold_in(key, 13), (), 0, BANDS_LAT)
    columns = lax.broadcasted_iota(jnp.int32, (NLON, NLAT), 0)
    rows = lax.broadcasted_iota(jnp.int32, (NLON, NLAT), 1)
    anchor = (columns % LON_DEV == 0) & (rows % LAT_DEV == 0)
    full = (columns // LON_DEV == full_lon) & (rows // LAT_DEV == full_lat)
    return jnp.where((values > 0) | anchor | full, 1, 0).astype(jnp.int32)


def draw_land_mask(key, part):
    return wet_table(key)


def draw_wet_counts(key, part):
    table = wet_table(key)
    tiles = jnp.sum(table.reshape(BANDS_LON, LON_DEV, BANDS_LAT, LAT_DEV), axis=(1, 3))
    return tiles.T.astype(jnp.int32)


def block_levels(own_key, extent, shards, least, top_value):
    def one(dim, parts):
        heights = jax.random.uniform(jax.random.fold_in(jax.random.fold_in(own_key, 6), dim), (parts,), jnp.float32, least / len(shards), top_value / len(shards))
        return jnp.repeat(jnp.exp(heights), extent[dim] // parts).reshape((-1,) + (1,) * (len(extent) - dim - 1))

    gain = one(*shards[0])
    for cut in shards[1:]:
        gain = gain * one(*cut)
    return gain


def gaussian(rng, dims, width, reach, cuts=(), kind=jnp.bfloat16):
    array = jax.random.normal(rng, dims, jnp.float32) * width
    if len(cuts) > 0:
        array = block_levels(rng, dims, cuts, -0.22, 0.18) * array
    return jnp.clip(array, min=-reach, max=reach).astype(kind)


def setup_inputs(seed: int = 0) -> dict:
    splits = jax.random.split(jax.random.key(seed), 12)
    sea_level = draw_sea_level(jax.random.fold_in(splits[11], 71), 0)
    east_velocity = gaussian(splits[1], (NLON, NLAT), 1.0, 6.0, ((0, 16), (1, 2)), jnp.float32)
    north_velocity = gaussian(splits[2], (NLON, NLAT), 1.0, 6.0, ((0, 16), (1, 2)), jnp.float32)
    depth = jnp.clip(jnp.exp(math.log(1.0) - 1.3862944 * jax.random.uniform(splits[3], (NLON, NLAT), jnp.float32) ** block_levels(splits[3], (NLON, NLAT), ((0, 16), (1, 2)), -0.2, 0.2)), 0.25, 1.0)
    land_mask = draw_land_mask(jax.random.fold_in(splits[11], 71), 0)
    wet_counts = draw_wet_counts(jax.random.fold_in(splits[11], 71), 0)
    loading_prev = gaussian(splits[6], (NLON, NLAT), 0.5, 4.0, ((0, 16), (1, 2)), jnp.float32)
    tide_amp = jnp.clip(jnp.exp(jax.random.uniform(splits[7], (CONSTITUENTS,), jnp.float32, math.log(0.3), math.log(1.0))), 0.3, 1.0)
    tide_phase = jnp.clip(jax.random.uniform(splits[8], (CONSTITUENTS,), jnp.float32, -3.140625, 3.140625), -3.140625, 3.140625)
    legendre = gaussian(splits[9], (M, NDEG, NLAT), NLAT ** -0.5, 0.375, ((0, 16), (2, 2)))
    love_factor = jnp.clip(jnp.exp(jax.random.uniform(splits[10], (NDEG,), jnp.float32, math.log(0.05), math.log(1.0))), 0.05, 1.0)
    return dict(sea_level=sea_level, east_velocity=east_velocity, north_velocity=north_velocity, depth=depth, land_mask=land_mask, wet_counts=wet_counts, loading_prev=loading_prev, tide_amp=tide_amp, tide_phase=tide_phase, legendre=legendre, love_factor=love_factor)


lat_edge = 1.3089969
courant = 0.4
friction = 0.02
rotation = 0.2
frequencies = (0.1405, 0.1454, 0.1379, 0.1458, 0.0729, 0.0676, 0.0725, 0.0649)
orders = (2, 2, 2, 2, 1, 1, 1, 1)

def latitude_of(rows, total_rows):
    return -lat_edge + 2.0 * lat_edge * (rows.astype(jnp.float32) + 0.5) / total_rows

def potential(columns, rows, moment, total_cols, total_rows, tide_amp, tide_phase):
    longitude = (2.0 * math.pi * (columns % total_cols).astype(jnp.float32) / total_cols)[:, None]
    latitude = latitude_of(rows, total_rows)[None, :]
    semi = jnp.cos(latitude) ** 2
    diurnal = jnp.sin(2.0 * latitude)
    field = jnp.zeros((columns.shape[0], rows.shape[0]), jnp.float32)
    for index in range(len(frequencies)):
        shape_term = semi if orders[index] == 2 else diurnal
        field = field + tide_amp[index] * shape_term * jnp.cos(frequencies[index] * moment + orders[index] * longitude + tide_phase[index])
    return field * (total_cols / 64.0)

def advance(state_x, static_x, forcing, latitude_x):
    height_x, east_x, north_x = (state_x[0], state_x[1], state_x[2])
    depth_x, wet_x, loading_x = (static_x[0], static_x[1], static_x[2])
    cosine = jnp.cos(latitude_x)[None, :]
    secant_cycle = (1.0 / jnp.cos(latitude_x[1:-1]))[None, :]
    secant_core = (1.0 / jnp.cos(latitude_x[2:-2]))[None, :]
    coriolis = (rotation * jnp.sin(latitude_x[2:-2]))[None, :]
    flux_east = depth_x * east_x
    flux_north = depth_x * north_x * cosine
    divergence = (flux_east[2:, 1:-1] - flux_east[:-2, 1:-1] + (flux_north[1:-1, 2:] - flux_north[1:-1, :-2])) * 0.5 * secant_cycle
    height_cycle = height_x[1:-1, 1:-1] - courant * divergence * wet_x[1:-1, 1:-1]
    pressure = height_cycle - forcing - loading_x[1:-1, 1:-1]
    slope_east = (pressure[2:, 1:-1] - pressure[:-2, 1:-1]) * 0.5 * secant_core
    slope_north = (pressure[1:-1, 2:] - pressure[1:-1, :-2]) * 0.5
    east = east_x[2:-2, 2:-2]
    north = north_x[2:-2, 2:-2]
    wet = wet_x[2:-2, 2:-2]
    east_next = wet * ((1.0 - friction) * east + courant * (coriolis * north - slope_east))
    north_next = wet * ((1.0 - friction) * north - courant * (coriolis * east + slope_north))
    return jnp.stack([height_cycle[1:-1, 1:-1], east_next, north_next])

def extend_grid(fields):
    wide = jnp.pad(fields, ((0, 0), (2, 2), (0, 0)), mode='wrap')
    return jnp.pad(wide, ((0, 0), (0, 0), (2, 2)))

def reference(sea_level, east_velocity, north_velocity, depth, land_mask, wet_counts, loading_prev, tide_amp, tide_phase, legendre, love_factor):
    wet = land_mask.astype(jnp.float32)
    static_x = extend_grid(jnp.stack([depth, wet, loading_prev]))
    state = jnp.stack([sea_level, east_velocity, north_velocity])
    latitude_x = latitude_of(jnp.arange(-2, NLAT + 2, dtype=jnp.int32), NLAT)
    columns = jnp.arange(-1, NLON + 1, dtype=jnp.int32)
    rows = jnp.arange(-1, NLAT + 1, dtype=jnp.int32)
    for moment in range(SUBSTEPS):
        forcing = potential(columns, rows, float(moment), NLON, NLAT, tide_amp, tide_phase)
        state = advance(extend_grid(state), static_x, forcing, latitude_x)
    height = state[0]
    mean_level = jnp.sum(wet * height) / jnp.sum(wet_counts.astype(jnp.float32))
    anomaly = wet * (height - mean_level)
    spectrum = jnp.fft.rfft(anomaly, axis=0)[:M] / math.sqrt(NLON)
    fourier = jnp.stack([jnp.real(spectrum), jnp.imag(spectrum)], axis=1).astype(jnp.bfloat16)

    def one_wave(pair):
        table, wave = pair
        coefficients = jnp.dot(wave, table.T, preferred_element_type=jnp.float32)
        scaled = (coefficients * love_factor[None, :]).astype(jnp.bfloat16)
        return jnp.dot(scaled, table, preferred_element_type=jnp.float32)
    synthesis = lax.map(one_wave, (legendre, fourier))
    padded = jnp.pad(synthesis, ((0, NLON // 2 + 1 - M), (0, 0), (0, 0)))
    spectral = lax.complex(padded[:, 0], padded[:, 1])
    self_attraction = (jnp.fft.irfft(spectral, n=NLON, axis=0) * math.sqrt(NLON)).astype(jnp.float32)
    return (state[0], state[1], state[2], self_attraction)
```

```python
import functools
import math

import jax
import jax.numpy as jnp
from jax import lax
from jax.experimental import pallas as pl
from jax.experimental.pallas import tpu as pltpu
from jax.sharding import PartitionSpec as P


SUBSTEPS = 4
MARGIN = 2 * SUBSTEPS

lat_edge = 1.3089969
courant = 0.4
friction = 0.02
rotation = 0.2
frequencies = (0.1405, 0.1454, 0.1379, 0.1458, 0.0729, 0.0676, 0.0725, 0.0649)
diurnal_from = 4

f32 = jnp.float32
bf16 = jnp.bfloat16
LANES = 128


def split_bf16(x):
    high = x.astype(bf16)
    return high, (x - high.astype(f32)).astype(bf16)


def call(kernel, out_shape, in_specs=None, scratch=(), vmem=None):
    params = pltpu.CompilerParams(vmem_limit_bytes=(vmem or 16) << 20)
    kwargs = {} if in_specs is None else {"in_specs": in_specs}
    return pl.pallas_call(
        kernel, out_shape=out_shape, scratch_shapes=scratch, compiler_params=params, **kwargs
    )


def shaped(*dims, dtype=f32):
    return jax.ShapeDtypeStruct(dims, dtype)


def pack_kernel(sea, east, north, depth, mask, loading, west_out, east_out, top_out, bottom_out):
    rows = sea.shape[0]
    for index, ref in enumerate((sea, east, north, depth, mask, loading)):
        cells = ref[...].astype(f32)
        west_out[index] = cells[:MARGIN]
        east_out[index] = cells[rows - MARGIN :]
        turned = cells.T
        top_out[index] = turned[turned.shape[0] - MARGIN :]
        bottom_out[index] = turned[:MARGIN]


def table_kernel(
    sizes,
    position,
    amp,
    phase,
    mask,
    legendre,
    forward,
    inverse,
    keep,
    send,
    forcing,
    latitude_out,
    legendre_out,
    sem,
):
    lon_dev, lat_dev, total_cols, total_rows, wave_dev, gens = sizes
    copy = pltpu.make_async_copy(legendre, legendre_out, sem)
    copy.start()
    lon_index = position[0]
    lat_index = position[1]
    chunk = 2 * wave_dev
    columns = lon_index * lon_dev + lax.broadcasted_iota(jnp.int32, (chunk, lon_dev), 1)
    line = lax.broadcasted_iota(jnp.int32, (chunk, lon_dev), 0)
    scale = 1.0 / math.sqrt(total_cols)
    chunks = 1 << len(gens)
    wet = mask[...].astype(bf16)
    for piece in range(chunks):
        offset = 0
        for place, gen in enumerate(gens):
            if piece >> (len(gens) - 1 - place) & 1:
                offset ^= gen
        owner = lon_index ^ offset
        wave = owner * wave_dev + (line >> 1)
        turns = (wave * columns + (line & 1) * (total_cols // 4)) % total_cols
        angle = (2.0 * math.pi / total_cols) * turns.astype(f32)
        wave_rows = scale * jnp.cos(angle)
        high, low = split_bf16(wave_rows)
        span = slice(piece * chunk, (piece + 1) * chunk)
        forward[span, :lon_dev] = high
        forward[span, lon_dev:] = low
        turned = wave_rows.T
        high_t, low_t = split_bf16(turned)
        inverse[:lon_dev, span] = high_t
        inverse[lon_dev:, span] = low_t
    half = chunks * chunk // 2
    twice = jnp.concatenate([wet, wet], axis=0)
    keep[...] = jnp.dot(forward[:half], twice, preferred_element_type=f32)
    send[...] = jnp.dot(forward[half:], twice, preferred_element_type=f32)

    wide = lon_dev + 2 * MARGIN
    lane = lax.broadcasted_iota(jnp.int32, (8, 2 * lat_dev), 1)
    row = jnp.where(lane < lat_dev + lat_dev // 2, lane, lane - 2 * lat_dev) + lat_index * lat_dev
    latitude = -lat_edge + 2.0 * lat_edge * (row.astype(f32) + 0.5) / total_rows
    inside = jnp.clip(latitude, -1.5, 1.5)
    cosine = jnp.cos(inside)
    latitude_out[0] = cosine
    latitude_out[1] = 1.0 / cosine
    latitude_out[2] = rotation * jnp.sin(inside)
    semi = jnp.cos(latitude) ** 2
    diurnal = jnp.sin(2.0 * latitude)

    count = len(frequencies)
    place = lax.broadcasted_iota(jnp.int32, (8, count), 1)
    moment = lax.broadcasted_iota(jnp.int32, (8, count), 0).astype(f32)
    omega = jnp.zeros((8, count), f32)
    for index in range(count):
        omega = jnp.where(place == index, frequencies[index], omega)
    argument = omega * moment + phase[...]
    strength = amp[...] * (total_cols / 64.0)
    real = strength * jnp.cos(argument)
    imag = strength * jnp.sin(argument)
    is_semi = place < diurnal_from

    def total(values, chosen):
        return jnp.sum(jnp.where(chosen, values, 0.0), axis=1, keepdims=True)

    semi_real = total(real, is_semi)
    semi_imag = total(imag, is_semi)
    diurnal_real = total(real, jnp.logical_not(is_semi))
    diurnal_imag = total(imag, jnp.logical_not(is_semi))
    spot = lax.broadcasted_iota(jnp.int32, (wide, 8), 0)
    order = 1 + (lax.broadcasted_iota(jnp.int32, (wide, 8), 1) & 1)
    spot = jnp.where(spot < lon_dev + MARGIN, spot, spot - wide) + lon_index * lon_dev
    spot = (spot * order + total_cols * 2) % total_cols
    longitude = (2.0 * math.pi / total_cols) * spot.astype(f32)
    cos_lon = jnp.cos(longitude)
    sin_lon = jnp.sin(longitude)
    cos_one, cos_two = cos_lon[:, 0:1], cos_lon[:, 1:2]
    sin_one, sin_two = sin_lon[:, 0:1], sin_lon[:, 1:2]
    for k in range(SUBSTEPS):
        at = slice(k, k + 1)
        along = cos_two * semi_real[at] - sin_two * semi_imag[at]
        across = cos_one * diurnal_real[at] - sin_one * diurnal_imag[at]
        forcing[k] = along * semi[0:1] + across * diurnal[0:1]
    copy.wait()


def step_kernel(
    sizes,
    flags,
    sea,
    east_in,
    north_in,
    depth_in,
    mask,
    loading_in,
    from_east,
    from_west,
    top,
    top_east,
    top_west,
    bottom,
    bottom_east,
    bottom_west,
    forcing,
    latitude,
    height_out,
    east_out,
    north_out,
    wet_height,
    wet_sum,
    static,
):
    lon_dev, lat_dev = sizes
    wide = lon_dev + 2 * MARGIN
    lanes = 2 * lat_dev
    has_top = flags[2] > 0
    has_bottom = flags[3] > 0
    middle = jnp.zeros((lat_dev - 2 * MARGIN, lon_dev), f32)
    lane = lax.broadcasted_iota(jnp.int32, (MARGIN, lon_dev), 1)
    from_right = lane < MARGIN

    def edges(index, above, below):
        north_rows = jnp.where(has_top, above[index], 0.0)
        south_rows = jnp.where(has_bottom, below[index], 0.0)
        return north_rows, south_rows

    fields = []
    for index, ref in enumerate((sea, east_in, north_in, depth_in, mask, loading_in)):
        own = ref[...].astype(f32)
        north_rows, south_rows = edges(index, top, bottom)
        side = jnp.concatenate([north_rows, middle, south_rows], axis=0).T
        ne, se = edges(index, top_east, bottom_east)
        nw, sw = edges(index, top_west, bottom_west)
        corner = jnp.concatenate(
            [jnp.where(from_right, ne, nw), middle, jnp.where(from_right, se, sw)], axis=0
        ).T
        left = jnp.concatenate([own, from_east[index], from_west[index]], axis=0)
        right = jnp.concatenate([side, corner[:MARGIN], corner[lon_dev - MARGIN :]], axis=0)
        fields.append(jnp.concatenate([left, right], axis=1))
    height, east, north, depth, wet, loading = fields
    static[0] = depth
    static[1] = wet
    static[2] = loading

    def along(f):
        return pltpu.roll(f, wide - 1, axis=0) - pltpu.roll(f, 1, axis=0)

    def across(f):
        return pltpu.roll(f, lanes - 1, axis=1) - pltpu.roll(f, 1, axis=1)

    cosine = latitude[0][0:1]
    secant = latitude[1][0:1]
    coriolis = latitude[2][0:1]
    for k in range(SUBSTEPS):
        depth = static[0]
        wet = static[1]
        divergence = (along(depth * east) + across(depth * north * cosine)) * 0.5 * secant
        height = height - courant * divergence * wet
        pressure = height - forcing[k] - static[2]
        slope_east = along(pressure) * 0.5 * secant
        slope_north = across(pressure) * 0.5
        east, north = (
            wet * ((1.0 - friction) * east + courant * (coriolis * north - slope_east)),
            wet * ((1.0 - friction) * north - courant * (coriolis * east + slope_north)),
        )
    core = height[:lon_dev, :lat_dev]
    height_out[...] = core
    east_out[...] = east[:lon_dev, :lat_dev]
    north_out[...] = north[:lon_dev, :lat_dev]
    product = core * static[1][:lon_dev, :lat_dev]
    wet_height[...] = product
    level = jnp.sum(jnp.sum(product, axis=0, keepdims=True), axis=1, keepdims=True)
    wet_sum[...] = jnp.broadcast_to(level, wet_sum.shape)


def fourier_kernel(wet_height, wet_sum, forward, keep, send):
    high, low = split_bf16(wet_height[...])
    top = jnp.concatenate([high, low], axis=1)
    under = jnp.concatenate([high, jnp.zeros_like(low)], axis=1)
    weights = jnp.concatenate([top, under], axis=0)
    half = keep.shape[0]
    cols = wet_height.shape[1]

    def transform(span):
        both = jnp.dot(forward[span], weights, preferred_element_type=f32)
        return both[:, :cols] + both[:, cols:]

    send[:half] = transform(slice(half, 2 * half))
    send[half:] = wet_sum[...]
    keep[...] = transform(slice(0, half))


GROUP = 4


def pair(legendre, wave, lat_axis):
    return jnp.concatenate([legendre[wave], legendre[wave + 1]], axis=1)


def analysis_kernel(
    sizes, keep, recv, wet_sum, wet_counts, wet_keep, wet_recv, legendre, out
):
    first, waves = sizes
    lat_dev = keep.shape[1]
    rows = keep.shape[0]
    counts = wet_counts[...].astype(f32)
    total = jnp.sum(jnp.sum(counts, axis=1, keepdims=True), axis=0, keepdims=True)
    mean = wet_sum[0:1, 0:1] / total
    lines = 2 * GROUP
    line = lax.broadcasted_iota(jnp.int32, (lines, lat_dev), 0) >> 1
    for group in range(waves // GROUP):
        span = slice(2 * first + group * lines, 2 * first + (group + 1) * lines)
        value = (keep[span] + recv[span]) - mean * (wet_keep[span] + wet_recv[span])
        value = value.astype(bf16).astype(f32)
        total_rows = None
        for step in range(0, GROUP, 2):
            wave = first + group * GROUP + step
            left = jnp.concatenate(
                [
                    jnp.where(line == step, value, 0.0),
                    jnp.where(line == step + 1, value, 0.0),
                ],
                axis=1,
            ).astype(bf16)
            part = lax.dot_general(
                left,
                pair(legendre, wave, lat_dev),
                (((1,), (1,)), ((), ())),
                preferred_element_type=f32,
            )
            total_rows = part if total_rows is None else total_rows + part
        out[group * lines : (group + 1) * lines] = total_rows


def synthesis_kernel(sizes, position, own, recv, love, legendre, *rest):
    first, waves, lat_dev, wave_dev = sizes
    out = rest[-1]
    lines = 2 * GROUP
    weights = love[...]
    base = 0
    if len(rest) == 2:
        base = rest[0].shape[0]
        out[:base] = rest[0][...]
    line = lax.broadcasted_iota(jnp.int32, (lines, lat_dev), 0) >> 1
    for group in range(waves // GROUP):
        span = slice(group * lines, (group + 1) * lines)
        scaled = (weights * (own[span] + recv[span])).astype(bf16)
        result = None
        for step in range(0, GROUP, 2):
            wave = first + group * GROUP + step
            both = jnp.dot(scaled, pair(legendre, wave, lat_dev), preferred_element_type=f32)
            left, right = both[:, :lat_dev], both[:, lat_dev:]
            if result is None:
                result = left
            else:
                result = jnp.where(line == step, left, result)
            result = jnp.where(line == step + 1, right, result)
        number = position[0] * wave_dev + first + group * GROUP + line
        result = jnp.where(number == 0, 1.0, 2.0) * result
        out[base + group * lines : base + (group + 1) * lines] = result


def inverse_kernel(inverse, near, far, out):
    lon_dev = out.shape[0]
    lat_dev = out.shape[1]
    half = near.shape[0]
    result = None
    for source, span in ((near, slice(0, half)), (far, slice(half, 2 * half))):
        high, low = split_bf16(source[...])
        both = jnp.dot(
            inverse[:, span], jnp.concatenate([high, low], axis=1), preferred_element_type=f32
        )
        part = both[:lon_dev, :lat_dev] + (both[lon_dev:, :lat_dev] + both[:lon_dev, lat_dev:])
        result = part if result is None else result + part
    out[...] = result


def shards(
    sea_level,
    east_velocity,
    north_velocity,
    depth,
    land_mask,
    wet_counts,
    loading_prev,
    tide_amp,
    tide_phase,
    legendre,
    love_factor,
):
    lon_dev, lat_dev = sea_level.shape
    wave_dev, degrees = legendre.shape[:2]
    lon_count = lax.axis_size("lon")
    lat_count = lax.axis_size("lat")
    total_cols = lon_dev * lon_count
    total_rows = lat_dev * lat_count
    lon_index = lax.axis_index("lon")
    lat_index = lax.axis_index("lat")
    bits = lon_count.bit_length() - 1
    lat_bits = lat_count.bit_length() - 1
    assert lon_count == 1 << bits and lat_count == 1 << lat_bits
    gens = [1] + [1 << b for b in (1, *range(bits - 1, 1, -1))][: bits - 1]
    position = jnp.stack(
        [
            lon_index,
            lat_index,
            (lat_index < lat_count - 1).astype(jnp.int32),
            (lat_index > 0).astype(jnp.int32),
        ]
    ).astype(jnp.int32)
    smem = pl.BlockSpec(memory_space=pltpu.SMEM)
    vmem = pl.BlockSpec(memory_space=pltpu.VMEM)
    anywhere = pl.BlockSpec(memory_space=pl.ANY)

    strip = shaped(6, MARGIN, LANES)
    west, east, top, bottom = call(pack_kernel, [strip] * 4)(
        sea_level, east_velocity, north_velocity, depth, land_mask, loading_prev
    )

    def shift(cells, lat_step, lon_step):
        pairs = []
        for a in range(lat_count):
            target = a ^ 1 if lat_step == "swap" else a + lat_step
            if not 0 <= target < lat_count:
                continue
            for b in range(lon_count):
                pairs.append((a * lon_count + b, target * lon_count + (b + lon_step) % lon_count))
        return lax.ppermute(cells, ("lat", "lon"), pairs)

    from_east = shift(west, 0, -1)
    from_west = shift(east, 0, 1)
    if lat_count == 2:
        facing = jnp.where(lat_index == 0, top, bottom)
        middle_strip = shift(facing, "swap", 0)
        east_strip = shift(facing, "swap", -1)
        west_strip = shift(facing, "swap", 1)
        above = (middle_strip, east_strip, west_strip)
        below = above
    else:
        above = (shift(bottom, -1, 0), shift(bottom, -1, -1), shift(bottom, -1, 1))
        below = (shift(top, 1, 0), shift(top, 1, -1), shift(top, 1, 1))

    chunk = 2 * wave_dev
    lines = chunk * lon_count
    half = lines // 2
    wide = lon_dev + 2 * MARGIN
    forward, inverse, wet_keep, wet_send, forcing, latitude, table = call(
        functools.partial(
            table_kernel, (lon_dev, lat_dev, total_cols, total_rows, wave_dev, tuple(gens))
        ),
        [
            shaped(lines, 2 * lon_dev, dtype=bf16),
            shaped(2 * lon_dev, lines, dtype=bf16),
            shaped(half, lat_dev),
            shaped(half, lat_dev),
            shaped(SUBSTEPS, wide, 2 * lat_dev),
            shaped(3, 8, 2 * lat_dev),
            pltpu.VMEM(legendre.shape, bf16),
        ],
        in_specs=[smem, vmem, vmem, vmem, anywhere],
        scratch=[pltpu.SemaphoreType.DMA],
        vmem=24,
    )(position, tide_amp[None], tide_phase[None], land_mask, legendre)

    def swap(cells, gen):
        return lax.ppermute(cells, "lon", [(i, i ^ gen) for i in range(lon_count)])

    wet_recv = swap(wet_send, gens[0])
    for gen in gens[1:]:
        part = wet_keep.shape[0] // 2
        wet_send = wet_keep[part:] + wet_recv[part:]
        wet_keep = wet_keep[:part] + wet_recv[:part]
        wet_recv = swap(wet_send, gen)

    height, east_new, north_new, wet_height, wet_sum = call(
        functools.partial(step_kernel, (lon_dev, lat_dev)),
        [shaped(lon_dev, lat_dev)] * 4 + [shaped(8, lat_dev)],
        in_specs=[smem] + [vmem] * 16,
        scratch=[pltpu.VMEM((3, wide, 2 * lat_dev), f32)],
    )(
        position,
        sea_level,
        east_velocity,
        north_velocity,
        depth,
        land_mask,
        loading_prev,
        from_east,
        from_west,
        *above,
        *below,
        forcing,
        latitude,
    )

    keep, send = call(
        fourier_kernel, [shaped(half, lat_dev), shaped(half + 8, lat_dev)]
    )(wet_height, wet_sum, forward)
    recv = swap(send, gens[0])
    level = wet_sum + recv[half:]
    joined = lat_count == 2 and bits > 1
    for place, gen in enumerate(gens[1:]):
        part = keep.shape[0] // 2
        send = jnp.concatenate([keep[part:] + recv[part : 2 * part], level], axis=0)
        keep = keep[:part] + recv[:part]
        recv = swap(send, gen)
        arrived = recv[part:]
        if place == 0 and joined:
            pairs = [
                (a * lon_count + b, (a ^ 1) * lon_count + b)
                for a in range(2)
                for b in range(lon_count)
            ]
            crossed = [(s, t ^ gen) for s, t in pairs]
            arrived = arrived + lax.ppermute(level, ("lat", "lon"), pairs)
            arrived = arrived + lax.ppermute(level, ("lat", "lon"), crossed)
        level = level + arrived
    if not joined:
        for b in range(lat_bits):
            level = level + lax.ppermute(
                level, "lat", [(i, i ^ (1 << b)) for i in range(lat_count)]
            )

    parts = 2
    waves = wave_dev // parts
    own = []
    for piece in range(parts):
        own.append(
            call(
                functools.partial(analysis_kernel, (piece * waves, waves)),
                shaped(2 * waves, degrees),
                in_specs=[vmem] * 7,
                vmem=16,
            )(keep, recv, level, wet_counts, wet_keep, wet_recv, table)
        )
    other = []
    for piece in range(parts):
        mine = own[piece]
        for b in range(lat_bits):
            swapped = lax.ppermute(mine, "lat", [(i, i ^ (1 << b)) for i in range(lat_count)])
            if b < lat_bits - 1:
                mine = mine + swapped
        own[piece] = mine
        other.append(swapped)
    spectra = ()
    for piece in range(parts):
        lead = sum(s.shape[0] for s in spectra)
        spectra = (
            call(
                functools.partial(
                    synthesis_kernel, (piece * waves, waves, lat_dev, wave_dev)
                ),
                shaped(lead + 2 * waves, lat_dev),
                in_specs=[smem] + [vmem] * (4 + len(spectra)),
                vmem=16,
            )(position, own[piece], other[piece], love_factor[None], table, *spectra),
        )
    near = spectra[0]
    for gen in gens[:0:-1]:
        near = jnp.concatenate([near, swap(near, gen)], axis=0)
    far = swap(near, gens[0])
    loading_new = call(inverse_kernel, shaped(lon_dev, lat_dev))(inverse, near, far)
    return (height, east_new, north_new, loading_new)


def solution(mesh):
    tile = P("lon", "lat")
    return jax.shard_map(
        shards,
        mesh=mesh,
        in_specs=(tile,) * 5 + (P(), tile, P(), P(), P("lon", None, "lat"), P()),
        out_specs=(tile,) * 4,
        check_vma=False,
    )
```

```python
import functools
import math

import jax
import jax.numpy as jnp
from jax import lax
from jax.experimental import pallas as pl
from jax.experimental.pallas import tpu as pltpu
from jax.sharding import PartitionSpec as P


SUBSTEPS = 4
MARGIN = 2 * SUBSTEPS

lat_edge = 1.3089969
courant = 0.4
friction = 0.02
rotation = 0.2
frequencies = (0.1405, 0.1454, 0.1379, 0.1458, 0.0729, 0.0676, 0.0725, 0.0649)
diurnal_from = 4

f32 = jnp.float32
bf16 = jnp.bfloat16
LANES = 128


def split_bf16(x):
    high = x.astype(bf16)
    return high, (x - high.astype(f32)).astype(bf16)


def call(kernel, out_shape, in_specs=None, scratch=(), vmem=None):
    params = pltpu.CompilerParams(vmem_limit_bytes=(vmem or 16) << 20)
    kwargs = {} if in_specs is None else {"in_specs": in_specs}
    return pl.pallas_call(
        kernel, out_shape=out_shape, scratch_shapes=scratch, compiler_params=params, **kwargs
    )


def shaped(*dims, dtype=f32):
    return jax.ShapeDtypeStruct(dims, dtype)


def fetch(source, first, target, sems):
    pieces = sems.shape[0]
    span = target.shape[0] // pieces
    copies = []
    for piece in range(pieces):
        taken = source.at[pl.ds(first + piece * span, span)]
        placed = target.at[pl.ds(piece * span, span)]
        copies.append(pltpu.make_async_copy(taken, placed, sems.at[piece]))
    return copies


def pack_kernel(sea, east, north, depth, mask, loading, own, near, away, *rest):
    strips = rest[:-3]
    wet, sems, wet_sem = rest[-3:]
    copies = [pltpu.make_async_copy(mask, wet, wet_sem)]
    for index, ref in ((0, sea), (1, east), (2, north), (3, depth), (5, loading)):
        copies.append(pltpu.make_async_copy(ref, own.at[index], sems.at[index]))
    for copy in copies:
        copy.start()
    odd = (lax.axis_index("lon") & 1) > 0
    lat_index = lax.axis_index("lat")
    rows, lat_dev = sea.shape
    for copy in copies:
        copy.wait()
    own[4] = wet[...].astype(f32)
    for index in range(6):
        cells = own[index]
        first = cells[:MARGIN]
        last = cells[rows - MARGIN :]
        near[index] = jnp.where(odd, first, last)
        away[index] = jnp.where(odd, last, first)
        turned = cells.T
        top = turned[lat_dev - MARGIN :]
        bottom = turned[:MARGIN]
        if len(strips) == 1:
            strips[0][index] = jnp.where(lat_index == 0, top, bottom)
        else:
            strips[0][index] = top
            strips[1][index] = bottom


def table_kernel(
    sizes,
    amp_in,
    phase_in,
    love_in,
    counts_in,
    legendre,
    own,
    forward,
    inverse,
    keep,
    send,
    forcing,
    latitude_out,
    love_out,
    counts_out,
    table,
    amp,
    phase,
    outer,
    sems,
    table_sems,
):
    lon_dev, lat_dev, total_cols, total_rows, wave_dev, gens = sizes
    pairs = ((amp_in, amp), (phase_in, phase), (love_in, love_out), (counts_in, counts_out))
    copies = [
        pltpu.make_async_copy(source, target, sems.at[place])
        for place, (source, target) in enumerate(pairs)
    ]
    large = fetch(legendre, 0, table, table_sems)
    for copy in copies + large:
        copy.start()
    lon_index = lax.axis_index("lon")
    lat_index = lax.axis_index("lat")
    chunk = 2 * wave_dev
    chunks = 1 << len(gens)
    scale = 1.0 / math.sqrt(total_cols)
    turn = 2.0 * math.pi / total_cols

    def trig(turns):
        angle = turn * (turns % total_cols).astype(f32)
        return jnp.cos(angle), jnp.sin(angle)

    columns = lon_index * lon_dev + lax.broadcasted_iota(jnp.int32, (wave_dev, lon_dev), 1)
    wave = lax.broadcasted_iota(jnp.int32, (wave_dev, lon_dev), 0)
    cos_in, sin_in = trig(wave * columns)
    cos_in = cos_in * scale
    sin_in = sin_in * scale
    columns = lon_index * lon_dev + lax.broadcasted_iota(jnp.int32, (chunks, lon_dev), 1)
    piece = lax.broadcasted_iota(jnp.int32, (chunks, lon_dev), 0)
    owner = jnp.zeros((chunks, lon_dev), jnp.int32) + lon_index
    for place, gen in enumerate(gens):
        owner = owner ^ (((piece >> (len(gens) - 1 - place)) & 1) * gen)
    cos_out, sin_out = trig(owner * wave_dev * columns)
    outer[0] = cos_out
    outer[1] = sin_out
    block = LANES // chunk

    def fill(index, _):
        rows = []
        for inner in range(block):
            at = pl.ds(index * block + inner, 1)
            cos_at, sin_at = outer[0, at], outer[1, at]
            rows.append(cos_at * cos_in - sin_at * sin_in)
            rows.append(-(sin_at * cos_in + cos_at * sin_in))
        rows = jnp.concatenate(rows, axis=0)
        high, low = split_bf16(rows)
        span = pl.ds(pl.multiple_of(index * LANES, LANES), LANES)
        forward[span, :lon_dev] = high
        forward[span, lon_dev:] = low
        high_t, low_t = split_bf16(rows.T)
        inverse[:lon_dev, span] = high_t
        inverse[lon_dev:, span] = low_t
        return 0

    lax.fori_loop(0, chunks // block, fill, 0)
    half = chunks * chunk // 2
    wet = own[4].astype(bf16)
    twice = jnp.concatenate([wet, wet], axis=0)
    send[...] = jnp.dot(forward[half:], twice, preferred_element_type=f32)
    keep[...] = jnp.dot(forward[:half], twice, preferred_element_type=f32)

    wide = lon_dev + 2 * MARGIN
    lane = lax.broadcasted_iota(jnp.int32, (8, 2 * lat_dev), 1)
    row = jnp.where(lane < lat_dev + lat_dev // 2, lane, lane - 2 * lat_dev) + lat_index * lat_dev
    latitude = -lat_edge + 2.0 * lat_edge * (row.astype(f32) + 0.5) / total_rows
    inside = jnp.clip(latitude, -1.5, 1.5)
    cosine = jnp.cos(inside)
    latitude_out[0] = cosine
    latitude_out[1] = 1.0 / cosine
    latitude_out[2] = rotation * jnp.sin(inside)
    semi = jnp.cos(latitude) ** 2
    diurnal = jnp.sin(2.0 * latitude)

    spot = lax.broadcasted_iota(jnp.int32, (8, wide), 1)
    order = 1 + (lax.broadcasted_iota(jnp.int32, (8, wide), 0) & 1)
    spot = jnp.where(spot < lon_dev + MARGIN, spot, spot - wide) + lon_index * lon_dev
    cos_lon, sin_lon = trig(spot * order + total_cols * 2)
    both = jnp.concatenate([cos_lon, sin_lon], axis=0).T
    cos_one, cos_two = both[:, 0:1], both[:, 1:2]
    sin_one, sin_two = both[:, 8:9], both[:, 9:10]

    count = len(frequencies)
    place = lax.broadcasted_iota(jnp.int32, (8, count), 1)
    moment = lax.broadcasted_iota(jnp.int32, (8, count), 0).astype(f32)
    omega = jnp.zeros((8, count), f32)
    for index in range(count):
        omega = jnp.where(place == index, frequencies[index], omega)
    for copy in copies:
        copy.wait()
    argument = omega * moment + phase[...]
    strength = amp[...] * (total_cols / 64.0)
    real = strength * jnp.cos(argument)
    imag = strength * jnp.sin(argument)
    is_semi = place < diurnal_from

    def total(values, chosen):
        return jnp.sum(jnp.where(chosen, values, 0.0), axis=1, keepdims=True)

    semi_real = total(real, is_semi)
    semi_imag = total(imag, is_semi)
    diurnal_real = total(real, jnp.logical_not(is_semi))
    diurnal_imag = total(imag, jnp.logical_not(is_semi))
    for k in range(SUBSTEPS):
        at = slice(k, k + 1)
        along = cos_two * semi_real[at] - sin_two * semi_imag[at]
        across = cos_one * diurnal_real[at] - sin_one * diurnal_imag[at]
        forcing[k] = along * semi[0:1] + across * diurnal[0:1]
    for copy in large:
        copy.wait()


def step_kernel(count, own, near, away, *rest):
    strips = rest[: 3 if count == 2 else 6]
    (
        forcing,
        latitude,
        legendre,
        height_out,
        east_out,
        north_out,
        wet_height,
        wet_sum,
        table,
        state,
        static,
        table_sems,
    ) = rest[len(strips) :]
    copies = fetch(legendre, table.shape[0], table, table_sems)
    for copy in copies:
        copy.start()
    above = strips[:3]
    below = strips[-3:]
    lon_dev, lat_dev = own.shape[1:]
    wide = lon_dev + 2 * MARGIN
    lanes = 2 * lat_dev
    lat_index = lax.axis_index("lat")
    odd = (lax.axis_index("lon") & 1) > 0
    has_top = lat_index < count - 1
    has_bottom = lat_index > 0
    middle = jnp.zeros((lat_dev - 2 * MARGIN, lon_dev), f32)
    lane = lax.broadcasted_iota(jnp.int32, (MARGIN, lon_dev), 1)
    use_near = (lane < MARGIN) != odd

    fields = []
    for index in range(6):
        cells = own[index]
        north_rows = jnp.where(has_top, above[0][index], 0.0)
        south_rows = jnp.where(has_bottom, below[0][index], 0.0)
        side = jnp.concatenate([north_rows, middle, south_rows], axis=0).T
        north_rows = jnp.where(use_near, above[1][index], above[2][index])
        south_rows = jnp.where(use_near, below[1][index], below[2][index])
        north_rows = jnp.where(has_top, north_rows, 0.0)
        south_rows = jnp.where(has_bottom, south_rows, 0.0)
        corner = jnp.concatenate([north_rows, middle, south_rows], axis=0).T
        from_east = jnp.where(odd, away[index], near[index])
        from_west = jnp.where(odd, near[index], away[index])
        left = jnp.concatenate([cells, from_east, from_west], axis=0)
        right = jnp.concatenate([side, corner[:MARGIN], corner[lon_dev - MARGIN :]], axis=0)
        fields.append(jnp.concatenate([left, right], axis=1))
    for index in range(3):
        state[index] = fields[index]
        static[index] = fields[3 + index]

    def along(f):
        return pltpu.roll(f, wide - 1, axis=0) - pltpu.roll(f, 1, axis=0)

    def across(f):
        return pltpu.roll(f, lanes - 1, axis=1) - pltpu.roll(f, 1, axis=1)

    cosine = latitude[0][0:1]
    secant = latitude[1][0:1]
    coriolis = latitude[2][0:1]

    def substep(k, _):
        east = state[1]
        north = state[2]
        depth = static[0]
        wet = static[1]
        divergence = (along(depth * east) + across(depth * north * cosine)) * 0.5 * secant
        height = state[0] - courant * divergence * wet
        state[0] = height
        pressure = height - forcing[k] - static[2]
        slope_east = along(pressure) * 0.5 * secant
        slope_north = across(pressure) * 0.5
        state[1] = wet * ((1.0 - friction) * east + courant * (coriolis * north - slope_east))
        state[2] = wet * ((1.0 - friction) * north - courant * (coriolis * east + slope_north))
        return 0

    lax.fori_loop(0, SUBSTEPS, substep, 0)
    core = state[0, :lon_dev, :lat_dev]
    height_out[...] = core
    east_out[...] = state[1, :lon_dev, :lat_dev]
    north_out[...] = state[2, :lon_dev, :lat_dev]
    product = core * own[4]
    wet_height[...] = product
    level = jnp.sum(jnp.sum(product, axis=0, keepdims=True), axis=1, keepdims=True)
    wet_sum[...] = jnp.broadcast_to(level, wet_sum.shape)
    for copy in copies:
        copy.wait()


def fourier_kernel(wet_height, wet_sum, forward, keep, send):
    high, low = split_bf16(wet_height[...])
    top = jnp.concatenate([high, low], axis=1)
    under = jnp.concatenate([high, jnp.zeros_like(low)], axis=1)
    weights = jnp.concatenate([top, under], axis=0)
    half = keep.shape[0]
    cols = wet_height.shape[1]

    def transform(span):
        both = jnp.dot(forward[span], weights, preferred_element_type=f32)
        return both[:, :cols] + both[:, cols:]

    send[:half] = transform(slice(half, 2 * half))
    send[half:] = wet_sum[...]
    keep[...] = transform(slice(0, half))


GROUP = 8


def pair(legendre, wave):
    return jnp.concatenate([legendre[wave], legendre[wave + 1]], axis=1)


def analysis_kernel(sizes, keep, recv, wet_sum, wet_counts, wet_keep, wet_recv, legendre, out):
    first, waves, wave_dev = sizes
    lat_dev = keep.shape[1]
    counts = wet_counts[...].astype(f32)
    total = jnp.sum(jnp.sum(counts, axis=1, keepdims=True), axis=0, keepdims=True)
    mean = wet_sum[0:1, 0:1] / total
    lines = 2 * GROUP
    line = lax.broadcasted_iota(jnp.int32, (lines, lat_dev), 0) & (GROUP - 1)
    for group in range(waves // GROUP):
        values = []
        for part in range(2):
            begin = part * wave_dev + first + group * GROUP
            span = slice(begin, begin + GROUP)
            values.append(
                (keep[span] + recv[span]) - mean * (wet_keep[span] + wet_recv[span])
            )
        value = jnp.concatenate(values, axis=0)
        result = None
        for step in range(0, GROUP, 2):
            wave = group * GROUP + step
            left = jnp.concatenate(
                [
                    jnp.where(line == step, value, 0.0).astype(bf16),
                    jnp.where(line == step + 1, value, 0.0).astype(bf16),
                ],
                axis=1,
            )
            term = lax.dot_general(
                left,
                pair(legendre, wave),
                (((1,), (1,)), ((), ())),
                preferred_element_type=f32,
            )
            result = term if result is None else result + term
        out[group * lines : (group + 1) * lines] = result.astype(out.dtype)


def synthesis_kernel(sizes, own, recv, love, legendre, *rest):
    first, waves, wave_dev = sizes
    out = rest[-1]
    lat_dev = out.shape[1]
    lines = 2 * GROUP
    line = lax.broadcasted_iota(jnp.int32, (lines, lat_dev), 0) & (GROUP - 1)
    base = lax.axis_index("lon") * wave_dev + first
    real, imag = [], []
    for group in range(waves // GROUP):
        span = slice(group * lines, (group + 1) * lines)
        total = own[span].astype(f32) + recv[span].astype(f32)
        scaled = (love[...] * total).astype(bf16)
        result = None
        for step in range(0, GROUP, 2):
            both = jnp.dot(
                scaled,
                pair(legendre, group * GROUP + step),
                preferred_element_type=f32,
            )
            left, right = both[:, :lat_dev], both[:, lat_dev:]
            result = left if result is None else jnp.where(line == step, left, result)
            result = jnp.where(line == step + 1, right, result)
        result = jnp.where(base + group * GROUP + line == 0, 1.0, 2.0) * result
        real.append(result[:GROUP])
        imag.append(result[GROUP:])
    if len(rest) == 2:
        half = rest[0].shape[0] // 2
        real.insert(0, rest[0][:half])
        imag.insert(0, rest[0][half:])
    out[...] = jnp.concatenate(real + imag, axis=0).astype(out.dtype)


def inverse_kernel(inverse, near, far, out):
    lon_dev = out.shape[0]
    half = near.shape[0]
    both = jnp.dot(inverse[:, :half], near[...], preferred_element_type=f32)
    both += jnp.dot(inverse[:, half:], far[...], preferred_element_type=f32)
    out[...] = both[:lon_dev] + both[lon_dev:]


def shards(
    sea_level,
    east_velocity,
    north_velocity,
    depth,
    land_mask,
    wet_counts,
    loading_prev,
    tide_amp,
    tide_phase,
    legendre,
    love_factor,
):
    lon_dev, lat_dev = sea_level.shape
    wave_dev, degrees = legendre.shape[:2]
    lon_count = lax.axis_size("lon")
    lat_count = lax.axis_size("lat")
    total_cols = lon_dev * lon_count
    total_rows = lat_dev * lat_count
    bits = lon_count.bit_length() - 1
    lat_bits = lat_count.bit_length() - 1
    assert lon_count == 1 << bits and lat_count == 1 << lat_bits
    gens = [1] + [(1 << b) ^ 1 for b in (1, *range(bits - 1, 1, -1))][: bits - 1]
    vmem = pl.BlockSpec(memory_space=pltpu.VMEM)
    hbm = pl.BlockSpec(memory_space=pltpu.HBM)

    strip = shaped(6, MARGIN, LANES)

    def stay_put(cells):
        return pltpu.with_memory_space_constraint(cells, pltpu.HBM)

    own, near, away, *strips = call(
        pack_kernel,
        [shaped(6, lon_dev, lat_dev), strip, strip] + [strip] * (1 if lat_count == 2 else 2),
        in_specs=[hbm] * 6,
        scratch=[
            pltpu.VMEM((lon_dev, lat_dev), jnp.int32),
            pltpu.SemaphoreType.DMA((6,)),
            pltpu.SemaphoreType.DMA,
        ],
    )(*map(stay_put, (sea_level, east_velocity, north_velocity, depth, land_mask, loading_prev)))

    def stay(b):
        return b

    def nearby(b):
        return b ^ 1

    def beyond(b):
        return (b + 1 if b & 1 else b - 1) % lon_count

    def shift(cells, lat_step, move):
        pairs = []
        for a in range(lat_count):
            target = a ^ 1 if lat_step is None else a + lat_step
            if 0 <= target < lat_count:
                for b in range(lon_count):
                    pairs.append((a * lon_count + b, target * lon_count + move(b)))
        return lax.ppermute(cells, ("lat", "lon"), pairs)

    moves = (stay, nearby, beyond)
    away = shift(away, 0, beyond)
    sources = [(None, strips[0])] if lat_count == 2 else [(-1, strips[1]), (1, strips[0])]
    strips = []
    for lat_step, source in sources:
        for move in moves:
            strips.append(shift(source, lat_step, move))
    near = shift(near, 0, nearby)

    chunk = 2 * wave_dev
    lines = chunk * lon_count
    half = lines // 2
    wide = lon_dev + 2 * MARGIN
    table_shape = pltpu.VMEM((wave_dev // 2, *legendre.shape[1:]), bf16)
    forward, inverse, wet_keep, wet_send, forcing, latitude, love, counts, table_0 = call(
        functools.partial(
            table_kernel, (lon_dev, lat_dev, total_cols, total_rows, wave_dev, tuple(gens))
        ),
        [
            shaped(lines, 2 * lon_dev, dtype=bf16),
            shaped(2 * lon_dev, lines, dtype=bf16),
            shaped(half, lat_dev),
            shaped(half, lat_dev),
            shaped(SUBSTEPS, wide, 2 * lat_dev),
            shaped(3, 8, 2 * lat_dev),
            shaped(1, degrees),
            shaped(*wet_counts.shape, dtype=jnp.int32),
            table_shape,
        ],
        in_specs=[hbm] * 5 + [vmem],
        scratch=[
            pltpu.VMEM((1, len(frequencies)), f32),
            pltpu.VMEM((1, len(frequencies)), f32),
            pltpu.VMEM((2, lon_count, lon_dev), f32),
            pltpu.SemaphoreType.DMA((4,)),
            pltpu.SemaphoreType.DMA((4,)),
        ],
    )(
        stay_put(tide_amp[None]),
        stay_put(tide_phase[None]),
        stay_put(love_factor[None]),
        stay_put(wet_counts),
        stay_put(legendre),
        own,
    )

    def swap(cells, gen):
        return lax.ppermute(cells, "lon", [(i, i ^ gen) for i in range(lon_count)])

    wet_recv = swap(wet_send, gens[0])
    for gen in gens[1:]:
        part = wet_keep.shape[0] // 2
        wet_send = wet_keep[part:] + wet_recv[part:]
        wet_keep = wet_keep[:part] + wet_recv[:part]
        wet_recv = swap(wet_send, gen)

    height, east_new, north_new, wet_height, wet_sum, table_1 = call(
        functools.partial(step_kernel, lat_count),
        [shaped(lon_dev, lat_dev)] * 4 + [shaped(8, lat_dev), table_shape],
        in_specs=[vmem] * (5 + len(strips)) + [hbm],
        scratch=[
            pltpu.VMEM((3, wide, 2 * lat_dev), f32),
            pltpu.VMEM((3, wide, 2 * lat_dev), f32),
            pltpu.SemaphoreType.DMA((4,)),
        ],
    )(own, near, away, *strips, forcing, latitude, stay_put(legendre))

    keep, send = call(
        fourier_kernel, [shaped(half, lat_dev), shaped(half + 8, lat_dev)]
    )(wet_height, wet_sum, forward)
    recv = swap(send, gens[0])
    level = wet_sum + recv[half:]
    joined = lat_count == 2 and bits > 1
    for place, gen in enumerate(gens[1:]):
        part = keep.shape[0] // 2
        send = jnp.concatenate([keep[part:] + recv[part : 2 * part], level], axis=0)
        keep = keep[:part] + recv[:part]
        recv = swap(send, gen)
        arrived = recv[part:]
        if place == 0 and joined:
            arrived = arrived + shift(level, None, stay)
            arrived = arrived + shift(level, None, lambda b: b ^ gen)
        level = level + arrived
    if not joined:
        for b in range(lat_bits):
            level = level + lax.ppermute(
                level, "lat", [(i, i ^ (1 << b)) for i in range(lat_count)]
            )

    tables = (table_0, table_1)
    parts = len(tables)
    waves = wave_dev // parts
    sums = []
    for piece in range(parts):
        mine = call(
            functools.partial(analysis_kernel, (piece * waves, waves, wave_dev)),
            shaped(2 * waves, degrees),
            in_specs=[vmem] * 7,
        )(keep, recv, level, counts, wet_keep, wet_recv, tables[piece])
        for b in range(lat_bits):
            other = lax.ppermute(mine, "lat", [(i, i ^ (1 << b)) for i in range(lat_count)])
            if b < lat_bits - 1:
                mine = mine + other
        sums.append((mine, other))
    spectra = ()
    for piece in range(parts):
        last = piece == parts - 1
        spectra = (
            call(
                functools.partial(synthesis_kernel, (piece * waves, waves, wave_dev)),
                shaped(2 * waves * (piece + 1), lat_dev, dtype=bf16 if last else f32),
                in_specs=[vmem] * (4 + len(spectra)),
            )(*sums[piece], love, tables[piece], *spectra),
        )
    near = spectra[0]
    for gen in gens[:0:-1]:
        near = jnp.concatenate([near, swap(near, gen)], axis=0)
    far = swap(near, gens[0])
    loading_new = call(inverse_kernel, shaped(lon_dev, lat_dev))(inverse, near, far)
    return (height, east_new, north_new, loading_new)


def solution(mesh):
    tile = P("lon", "lat")
    return jax.shard_map(
        shards,
        mesh=mesh,
        in_specs=(tile,) * 5 + (P(), tile, P(), P(), P("lon", None, "lat"), P()),
        out_specs=(tile,) * 4,
        check_vma=False,
    )
```

```python
import functools
import math

import jax
import jax.numpy as jnp
from jax import lax
from jax.experimental import pallas as pl
from jax.experimental.pallas import tpu as pltpu
from jax.sharding import PartitionSpec as P


SUBSTEPS = 4
MARGIN = 2 * SUBSTEPS

lat_edge = 1.3089969
courant = 0.4
friction = 0.02
rotation = 0.2
frequencies = (0.1405, 0.1454, 0.1379, 0.1458, 0.0729, 0.0676, 0.0725, 0.0649)
diurnal_from = 4

f32 = jnp.float32
bf16 = jnp.bfloat16
LANES = 128


def split_bf16(x):
    high = x.astype(bf16)
    return high, (x - high.astype(f32)).astype(bf16)


def call(kernel, out_shape, in_specs=None, scratch=(), vmem=None):
    params = pltpu.CompilerParams(vmem_limit_bytes=(vmem or 16) << 20)
    kwargs = {} if in_specs is None else {"in_specs": in_specs}
    return pl.pallas_call(
        kernel, out_shape=out_shape, scratch_shapes=scratch, compiler_params=params, **kwargs
    )


def shaped(*dims, dtype=f32):
    return jax.ShapeDtypeStruct(dims, dtype)


def fetch(source, first, target, sems):
    pieces = sems.shape[0]
    span = target.shape[0] // pieces
    copies = []
    for piece in range(pieces):
        taken = source.at[pl.ds(first + piece * span, span)]
        placed = target.at[pl.ds(piece * span, span)]
        copies.append(pltpu.make_async_copy(taken, placed, sems.at[piece]))
    return copies


def pack_kernel(sea, east, north, depth, mask, loading, own, near, away, *rest):
    strips = rest[:-3]
    wet, sems, wet_sem = rest[-3:]
    copies = [pltpu.make_async_copy(mask, wet, wet_sem)]
    for index, ref in ((0, sea), (1, east), (2, north), (3, depth), (5, loading)):
        copies.append(pltpu.make_async_copy(ref, own.at[index], sems.at[index]))
    for copy in copies:
        copy.start()
    odd = (lax.axis_index("lon") & 1) > 0
    lat_index = lax.axis_index("lat")
    rows, lat_dev = sea.shape
    for copy in copies:
        copy.wait()
    filled = wet[...].astype(f32)
    own[4] = filled
    for index in range(rows // MARGIN):
        near[6 + index] = filled[index * MARGIN : (index + 1) * MARGIN]
    for index in range(6):
        cells = own[index]
        first = cells[:MARGIN]
        last = cells[rows - MARGIN :]
        near[index] = jnp.where(odd, first, last)
        away[index] = jnp.where(odd, last, first)
        turned = cells.T
        top = turned[lat_dev - MARGIN :]
        bottom = turned[:MARGIN]
        if len(strips) == 1:
            strips[0][index] = jnp.where(lat_index == 0, top, bottom)
        else:
            strips[0][index] = top
            strips[1][index] = bottom


def turns_trig(turns, total_cols):
    angle = (2.0 * math.pi / total_cols) * (turns % total_cols).astype(f32)
    return jnp.cos(angle), jnp.sin(angle)


def owners(piece, lon_index, gens):
    owner = jnp.zeros(piece.shape, jnp.int32) + lon_index
    for place, gen in enumerate(gens):
        owner = owner ^ (((piece >> (len(gens) - 1 - place)) & 1) * gen)
    return owner


def table_kernel(
    sizes,
    amp_in,
    phase_in,
    love_in,
    counts_in,
    legendre,
    own,
    near,
    forward,
    inverse,
    wet_pair,
    forcing,
    latitude_out,
    love_out,
    counts_out,
    table,
    amp,
    phase,
    outer,
    sems,
    table_sems,
):
    lon_dev, lat_dev, total_cols, total_rows, wave_dev, gens = sizes
    pairs = ((amp_in, amp), (phase_in, phase), (love_in, love_out), (counts_in, counts_out))
    copies = [
        pltpu.make_async_copy(source, target, sems.at[place])
        for place, (source, target) in enumerate(pairs)
    ]
    large = fetch(legendre, 0, table, table_sems)
    for copy in copies + large:
        copy.start()
    lon_index = lax.axis_index("lon")
    lat_index = lax.axis_index("lat")
    chunk = 2 * wave_dev
    chunks = 1 << len(gens)
    scale = 1.0 / math.sqrt(total_cols)

    def trig(turns):
        return turns_trig(turns, total_cols)

    columns = lon_index * lon_dev + lax.broadcasted_iota(jnp.int32, (wave_dev, lon_dev), 1)
    wave = lax.broadcasted_iota(jnp.int32, (wave_dev, lon_dev), 0)
    cos_in, sin_in = trig(wave * columns)
    cos_in = cos_in * scale
    sin_in = sin_in * scale
    columns = lon_index * lon_dev + lax.broadcasted_iota(jnp.int32, (chunks, lon_dev), 1)
    piece = lax.broadcasted_iota(jnp.int32, (chunks, lon_dev), 0)
    owner = owners(piece, lon_index, gens)
    cos_out, sin_out = trig(owner * wave_dev * columns)
    outer[0] = cos_out
    outer[1] = sin_out
    block = LANES // chunk

    def fill(index, _):
        rows = []
        for inner in range(block):
            at = pl.ds(index * block + inner, 1)
            cos_at, sin_at = outer[0, at], outer[1, at]
            rows.append(cos_at * cos_in - sin_at * sin_in)
            rows.append(-(sin_at * cos_in + cos_at * sin_in))
        rows = jnp.concatenate(rows, axis=0)
        high, low = split_bf16(rows)
        span = pl.ds(pl.multiple_of(index * LANES, LANES), LANES)
        forward[span, :lon_dev] = high
        forward[span, lon_dev:] = low
        high_t, low_t = split_bf16(rows.T)
        inverse[:lon_dev, span] = high_t
        inverse[lon_dev:, span] = low_t
        return 0

    lax.fori_loop(0, chunks // block, fill, 0)
    wet_pair[:lon_dev] = own[4].astype(bf16)
    for index in range(0, lon_dev // MARGIN, 2):
        both = jnp.concatenate([near[6 + index], near[7 + index]], axis=0)
        at = lon_dev + index * MARGIN
        wet_pair[at : at + 2 * MARGIN] = both.astype(bf16)

    wide = lon_dev + 2 * MARGIN
    lane = lax.broadcasted_iota(jnp.int32, (8, 2 * lat_dev), 1)
    row = jnp.where(lane < lat_dev + lat_dev // 2, lane, lane - 2 * lat_dev) + lat_index * lat_dev
    latitude = -lat_edge + 2.0 * lat_edge * (row.astype(f32) + 0.5) / total_rows
    inside = jnp.clip(latitude, -1.5, 1.5)
    cosine = jnp.cos(inside)
    latitude_out[0] = cosine
    latitude_out[1] = 1.0 / cosine
    latitude_out[2] = rotation * jnp.sin(inside)
    semi = jnp.cos(latitude) ** 2
    diurnal = jnp.sin(2.0 * latitude)

    spot = lax.broadcasted_iota(jnp.int32, (8, wide), 1)
    order = 1 + (lax.broadcasted_iota(jnp.int32, (8, wide), 0) & 1)
    spot = jnp.where(spot < lon_dev + MARGIN, spot, spot - wide) + lon_index * lon_dev
    cos_lon, sin_lon = trig(spot * order + total_cols * 2)
    both = jnp.concatenate([cos_lon, sin_lon], axis=0).T
    cos_one, cos_two = both[:, 0:1], both[:, 1:2]
    sin_one, sin_two = both[:, 8:9], both[:, 9:10]

    count = len(frequencies)
    place = lax.broadcasted_iota(jnp.int32, (8, count), 1)
    moment = lax.broadcasted_iota(jnp.int32, (8, count), 0).astype(f32)
    omega = jnp.zeros((8, count), f32)
    for index in range(count):
        omega = jnp.where(place == index, frequencies[index], omega)
    for copy in copies:
        copy.wait()
    argument = omega * moment + phase[...]
    strength = amp[...] * (total_cols / 64.0)
    real = strength * jnp.cos(argument)
    imag = strength * jnp.sin(argument)
    is_semi = place < diurnal_from

    def total(values, chosen):
        return jnp.sum(jnp.where(chosen, values, 0.0), axis=1, keepdims=True)

    semi_real = total(real, is_semi)
    semi_imag = total(imag, is_semi)
    diurnal_real = total(real, jnp.logical_not(is_semi))
    diurnal_imag = total(imag, jnp.logical_not(is_semi))
    for k in range(SUBSTEPS):
        at = slice(k, k + 1)
        along = cos_two * semi_real[at] - sin_two * semi_imag[at]
        across = cos_one * diurnal_real[at] - sin_one * diurnal_imag[at]
        forcing[k] = along * semi[0:1] + across * diurnal[0:1]
    for copy in large:
        copy.wait()


def mask_kernel(sizes, pair, far, keep, send):
    lon_dev, total_cols, wave_dev, gens = sizes
    lon_index = lax.axis_index("lon")
    chunks = 1 << (len(gens) - 2)
    scale = 1.0 / math.sqrt(total_cols)
    column = lax.broadcasted_iota(jnp.int32, (wave_dev, lon_dev), 1)
    wave = lax.broadcasted_iota(jnp.int32, (wave_dev, lon_dev), 0)
    spot = lax.broadcasted_iota(jnp.int32, (chunks, lon_dev), 1)
    piece = lax.broadcasted_iota(jnp.int32, (chunks, lon_dev), 0)
    owner = owners(piece, lon_index, gens[2:])
    result = None
    for source, other in ((pair, 0), (far, gens[1])):
        for at, offset in ((0, other), (1, other ^ gens[0])):
            start = (lon_index ^ offset) * lon_dev
            cos_in, sin_in = turns_trig(wave * (column + start), total_cols)
            cos_in = cos_in * scale
            sin_in = sin_in * scale
            cos_out, sin_out = turns_trig(owner * wave_dev * (spot + start), total_cols)
            rows = []
            for index in range(chunks):
                cos_at, sin_at = cos_out[index : index + 1], sin_out[index : index + 1]
                rows.append(cos_at * cos_in - sin_at * sin_in)
                rows.append(-(sin_at * cos_in + cos_at * sin_in))
            high, low = split_bf16(jnp.concatenate(rows, axis=0))
            wet = source[at * lon_dev : (at + 1) * lon_dev]
            term = jnp.dot(
                jnp.concatenate([high, low], axis=1),
                jnp.concatenate([wet, wet], axis=0),
                preferred_element_type=f32,
            )
            result = term if result is None else result + term
    half = keep.shape[0]
    keep[...] = result[:half]
    send[...] = result[half:]


def step_kernel(count, own, near, away, *rest):
    strips = rest[: 3 if count == 2 else 6]
    (
        forcing,
        latitude,
        legendre,
        height_out,
        east_out,
        north_out,
        wet_height,
        wet_sum,
        table,
        state,
        static,
        table_sems,
    ) = rest[len(strips) :]
    copies = fetch(legendre, table.shape[0], table, table_sems)
    for copy in copies:
        copy.start()
    above = strips[:3]
    below = strips[-3:]
    lon_dev, lat_dev = own.shape[1:]
    wide = lon_dev + 2 * MARGIN
    lanes = 2 * lat_dev
    lat_index = lax.axis_index("lat")
    odd = (lax.axis_index("lon") & 1) > 0
    has_top = lat_index < count - 1
    has_bottom = lat_index > 0
    middle = jnp.zeros((lat_dev - 2 * MARGIN, lon_dev), f32)
    lane = lax.broadcasted_iota(jnp.int32, (MARGIN, lon_dev), 1)
    use_near = (lane < MARGIN) != odd

    fields = []
    for index in range(6):
        cells = own[index]
        north_rows = jnp.where(has_top, above[0][index], 0.0)
        south_rows = jnp.where(has_bottom, below[0][index], 0.0)
        side = jnp.concatenate([north_rows, middle, south_rows], axis=0).T
        north_rows = jnp.where(use_near, above[1][index], above[2][index])
        south_rows = jnp.where(use_near, below[1][index], below[2][index])
        north_rows = jnp.where(has_top, north_rows, 0.0)
        south_rows = jnp.where(has_bottom, south_rows, 0.0)
        corner = jnp.concatenate([north_rows, middle, south_rows], axis=0).T
        from_east = jnp.where(odd, away[index], near[index])
        from_west = jnp.where(odd, near[index], away[index])
        left = jnp.concatenate([cells, from_east, from_west], axis=0)
        right = jnp.concatenate([side, corner[:MARGIN], corner[lon_dev - MARGIN :]], axis=0)
        fields.append(jnp.concatenate([left, right], axis=1))
    for index in range(3):
        state[index] = fields[index]
        static[index] = fields[3 + index]

    def along(f):
        return pltpu.roll(f, wide - 1, axis=0) - pltpu.roll(f, 1, axis=0)

    def across(f):
        return pltpu.roll(f, lanes - 1, axis=1) - pltpu.roll(f, 1, axis=1)

    cosine = latitude[0][0:1]
    secant = latitude[1][0:1]
    coriolis = latitude[2][0:1]

    def substep(k, _):
        east = state[1]
        north = state[2]
        depth = static[0]
        wet = static[1]
        divergence = (along(depth * east) + across(depth * north * cosine)) * 0.5 * secant
        height = state[0] - courant * divergence * wet
        state[0] = height
        pressure = height - forcing[k] - static[2]
        slope_east = along(pressure) * 0.5 * secant
        slope_north = across(pressure) * 0.5
        state[1] = wet * ((1.0 - friction) * east + courant * (coriolis * north - slope_east))
        state[2] = wet * ((1.0 - friction) * north - courant * (coriolis * east + slope_north))
        return 0

    lax.fori_loop(0, SUBSTEPS, substep, 0)
    core = state[0, :lon_dev, :lat_dev]
    height_out[...] = core
    east_out[...] = state[1, :lon_dev, :lat_dev]
    north_out[...] = state[2, :lon_dev, :lat_dev]
    product = core * own[4]
    wet_height[...] = product
    level = jnp.sum(jnp.sum(product, axis=0, keepdims=True), axis=1, keepdims=True)
    wet_sum[...] = jnp.broadcast_to(level, wet_sum.shape)
    for copy in copies:
        copy.wait()


def fourier_kernel(wet_height, wet_sum, forward, keep, send):
    high, low = split_bf16(wet_height[...])
    top = jnp.concatenate([high, low], axis=1)
    under = jnp.concatenate([high, jnp.zeros_like(low)], axis=1)
    weights = jnp.concatenate([top, under], axis=0)
    half = keep.shape[0]
    cols = wet_height.shape[1]

    def transform(span):
        both = jnp.dot(forward[span], weights, preferred_element_type=f32)
        return both[:, :cols] + both[:, cols:]

    send[:half] = transform(slice(half, 2 * half))
    send[half:] = wet_sum[...]
    keep[...] = transform(slice(0, half))


GROUP = 8


def pair(legendre, wave):
    return jnp.concatenate([legendre[wave], legendre[wave + 1]], axis=1)


def analysis_kernel(first, keep, recv, wet_keep, wet_sum, wet_counts, table, out, *sent):
    lat_dev = keep.shape[1]
    rows = keep.shape[0]
    counts = wet_counts[...].astype(f32)
    total = jnp.sum(jnp.sum(counts, axis=1, keepdims=True), axis=0, keepdims=True)
    mean = wet_sum[0:1, 0:1] / total
    lines = 2 * GROUP
    line = lax.broadcasted_iota(jnp.int32, (lines, lat_dev), 0) & (GROUP - 1)
    for group in range(table.shape[0] // GROUP):
        values = []
        for begin in (first + group * GROUP, rows // 2 + first + group * GROUP):
            span = slice(begin, begin + GROUP)
            wet_span = slice(rows + begin, rows + begin + GROUP)
            values.append((keep[span] + recv[span]) - mean * (wet_keep[span] + recv[wet_span]))
        value = jnp.concatenate(values, axis=0)
        result = None
        for step in range(0, GROUP, 2):
            left = jnp.concatenate(
                [
                    jnp.where(line == step, value, 0.0).astype(bf16),
                    jnp.where(line == step + 1, value, 0.0).astype(bf16),
                ],
                axis=1,
            )
            term = lax.dot_general(
                left,
                pair(table, group * GROUP + step),
                (((1,), (1,)), ((), ())),
                preferred_element_type=f32,
            )
            result = term if result is None else result + term
        for target in (out, *sent):
            target[group * lines : (group + 1) * lines] = result.astype(target.dtype)


def synthesis_kernel(sizes, own, recv, love, table, *rest):
    first, wave_dev = sizes
    out = rest[-1]
    lead = rest[:-1]
    lat_dev = out.shape[1]
    lines = 2 * GROUP
    line = lax.broadcasted_iota(jnp.int32, (lines, lat_dev), 0) & (GROUP - 1)
    base = lax.axis_index("lon") * wave_dev + first
    real, imag = [], []
    for group in range(table.shape[0] // GROUP):
        span = slice(group * lines, (group + 1) * lines)
        total = own[span].astype(f32) + recv[span].astype(f32)
        scaled = (love[...] * total).astype(bf16)
        result = None
        for step in range(0, GROUP, 2):
            both = jnp.dot(scaled, pair(table, group * GROUP + step), preferred_element_type=f32)
            left, right = both[:, :lat_dev], both[:, lat_dev:]
            result = left if result is None else jnp.where(line == step, left, result)
            result = jnp.where(line == step + 1, right, result)
        result = jnp.where(base + group * GROUP + line == 0, 1.0, 2.0) * result
        real.append(result[:GROUP])
        imag.append(result[GROUP:])
    if lead:
        half = lead[0].shape[0] // 2
        real.insert(0, lead[0][:half])
        imag.insert(0, lead[0][half:])
    out[...] = jnp.concatenate(real + imag, axis=0).astype(out.dtype)


def inverse_kernel(inverse, near, far, out):
    lon_dev = out.shape[0]
    half = near.shape[0]
    both = jnp.dot(inverse[:, :half], near[...], preferred_element_type=f32)
    both += jnp.dot(inverse[:, half:], far[...], preferred_element_type=f32)
    out[...] = both[:lon_dev] + both[lon_dev:]


def shards(
    sea_level,
    east_velocity,
    north_velocity,
    depth,
    land_mask,
    wet_counts,
    loading_prev,
    tide_amp,
    tide_phase,
    legendre,
    love_factor,
):
    lon_dev, lat_dev = sea_level.shape
    wave_dev, degrees = legendre.shape[:2]
    lon_count = lax.axis_size("lon")
    lat_count = lax.axis_size("lat")
    total_cols = lon_dev * lon_count
    total_rows = lat_dev * lat_count
    bits = lon_count.bit_length() - 1
    lat_bits = lat_count.bit_length() - 1
    assert lon_count == 1 << bits and lat_count == 1 << lat_bits
    gens = [1] + [(1 << b) ^ 1 for b in (1, *range(bits - 1, 1, -1))][: bits - 1]
    vmem = pl.BlockSpec(memory_space=pltpu.VMEM)
    hbm = pl.BlockSpec(memory_space=pltpu.HBM)

    strip = shaped(6, MARGIN, LANES)

    def stay_put(cells):
        return pltpu.with_memory_space_constraint(cells, pltpu.HBM)

    own, near, away, *strips = call(
        pack_kernel,
        [shaped(6, lon_dev, lat_dev), shaped(6 + lon_dev // MARGIN, MARGIN, LANES), strip] + [strip] * (1 if lat_count == 2 else 2),
        in_specs=[hbm] * 6,
        scratch=[
            pltpu.VMEM((lon_dev, lat_dev), jnp.int32),
            pltpu.SemaphoreType.DMA((6,)),
            pltpu.SemaphoreType.DMA,
        ],
    )(*map(stay_put, (sea_level, east_velocity, north_velocity, depth, land_mask, loading_prev)))

    def stay(b):
        return b

    def nearby(b):
        return b ^ 1

    def beyond(b):
        return (b + 1 if b & 1 else b - 1) % lon_count

    def shift(cells, lat_step, move):
        pairs = []
        for a in range(lat_count):
            target = a ^ 1 if lat_step is None else a + lat_step
            if 0 <= target < lat_count:
                for b in range(lon_count):
                    pairs.append((a * lon_count + b, target * lon_count + move(b)))
        return lax.ppermute(cells, ("lat", "lon"), pairs)

    moves = (stay, nearby, beyond)
    away = shift(away, 0, beyond)
    sources = [(None, strips[0])] if lat_count == 2 else [(-1, strips[1]), (1, strips[0])]
    strips = []
    for lat_step, source in sources:
        for move in moves:
            strips.append(shift(source, lat_step, move))
    near = shift(near, 0, nearby)

    chunk = 2 * wave_dev
    lines = chunk * lon_count
    half = lines // 2
    wide = lon_dev + 2 * MARGIN
    table = stay_put(legendre)
    table_shape = pltpu.VMEM((wave_dev // 2, *legendre.shape[1:]), bf16)
    forward, inverse, wet_pair, forcing, latitude, love, counts, table_0 = call(
        functools.partial(
            table_kernel, (lon_dev, lat_dev, total_cols, total_rows, wave_dev, tuple(gens))
        ),
        [
            shaped(lines, 2 * lon_dev, dtype=bf16),
            shaped(2 * lon_dev, lines, dtype=bf16),
            shaped(2 * lon_dev, lat_dev, dtype=bf16),
            shaped(SUBSTEPS, wide, 2 * lat_dev),
            shaped(3, 8, 2 * lat_dev),
            shaped(1, degrees),
            shaped(*wet_counts.shape, dtype=jnp.int32),
            table_shape,
        ],
        in_specs=[hbm] * 5 + [vmem] * 2,
        scratch=[
            pltpu.VMEM((1, len(frequencies)), f32),
            pltpu.VMEM((1, len(frequencies)), f32),
            pltpu.VMEM((2, lon_count, lon_dev), f32),
            pltpu.SemaphoreType.DMA((4,)),
            pltpu.SemaphoreType.DMA((4,)),
        ],
    )(
        stay_put(tide_amp[None]),
        stay_put(tide_phase[None]),
        stay_put(love_factor[None]),
        stay_put(wet_counts),
        table,
        own,
        near,
    )

    def swap(cells, gen):
        return lax.ppermute(cells, "lon", [(i, i ^ gen) for i in range(lon_count)])

    wet_far = swap(wet_pair, gens[1])

    height, east_new, north_new, wet_height, wet_sum, table_1 = call(
        functools.partial(step_kernel, lat_count),
        [shaped(lon_dev, lat_dev)] * 4 + [shaped(8, lat_dev), table_shape],
        in_specs=[vmem] * (5 + len(strips)) + [hbm],
        scratch=[
            pltpu.VMEM((3, wide, 2 * lat_dev), f32),
            pltpu.VMEM((3, wide, 2 * lat_dev), f32),
            pltpu.SemaphoreType.DMA((4,)),
        ],
    )(own, near, away, *strips, forcing, latitude, table)

    keep, send = call(
        fourier_kernel, [shaped(half, lat_dev), shaped(half + 8, lat_dev)]
    )(wet_height, wet_sum, forward)
    recv = swap(send, gens[0])
    wet_keep, wet_send = call(
        functools.partial(mask_kernel, (lon_dev, total_cols, wave_dev, tuple(gens))),
        [shaped(half // 4, lat_dev)] * 2,
    )(wet_pair, wet_far)
    wet_recv = swap(wet_send, gens[2])
    level = wet_sum + recv[half:]
    joined = lat_count == 2
    part = half // 2
    send = jnp.concatenate([keep[part:] + recv[part:half], level], axis=0)
    keep = keep[:part] + recv[:part]
    recv = swap(send, gens[1])
    arrived = recv[part:]
    if joined:
        arrived = arrived + shift(level, None, stay)
        arrived = arrived + shift(level, None, lambda b: b ^ gens[1])
    level = level + arrived
    for place, gen in enumerate(gens[2:]):
        part = keep.shape[0] // 2
        sends = [keep[part:] + recv[part : 2 * part]]
        keep = keep[:part] + recv[:part]
        if place > 0:
            sends.append(wet_keep[part:] + wet_recv[part : 2 * part])
            wet_keep = wet_keep[:part] + wet_recv[:part]
        recv = swap(jnp.concatenate([*sends, level], axis=0), gen)
        if place > 0:
            wet_recv = recv[part : 2 * part]
            level = level + recv[2 * part :]
        else:
            level = level + recv[part:]
    if not joined:
        for b in range(lat_bits):
            level = level + lax.ppermute(
                level, "lat", [(i, i ^ (1 << b)) for i in range(lat_count)]
            )

    tables = (table_0, table_1)
    parts = len(tables)
    waves = wave_dev // parts
    sums = []
    for piece in range(parts):
        mine, moving = call(
            functools.partial(analysis_kernel, piece * waves),
            [shaped(2 * waves, degrees), shaped(2 * waves, degrees, dtype=bf16)],
            in_specs=[vmem] * 6,
        )(keep, recv, wet_keep, level, counts, tables[piece])
        for b in range(lat_bits):
            other = lax.ppermute(moving, "lat", [(i, i ^ (1 << b)) for i in range(lat_count)])
            if b < lat_bits - 1:
                mine = mine + other.astype(f32)
                moving = mine.astype(bf16)
        sums.append((mine, other))
    spectra = ()
    for piece in range(parts):
        last = piece == parts - 1
        spectra = (
            call(
                functools.partial(synthesis_kernel, (piece * waves, wave_dev)),
                shaped(2 * waves * (piece + 1), lat_dev, dtype=bf16 if last else f32),
                in_specs=[vmem] * (4 + len(spectra)),
            )(*sums[piece], love, tables[piece], *spectra),
        )
    near = spectra[0]
    for gen in gens[:0:-1]:
        near = jnp.concatenate([near, swap(near, gen)], axis=0)
    far = swap(near, gens[0])
    loading_new = call(inverse_kernel, shaped(lon_dev, lat_dev))(inverse, near, far)
    return (height, east_new, north_new, loading_new)


def solution(mesh):
    tile = P("lon", "lat")
    return jax.shard_map(
        shards,
        mesh=mesh,
        in_specs=(tile,) * 5 + (P(), tile, P(), P(), P("lon", None, "lat"), P()),
        out_specs=(tile,) * 4,
        check_vma=False,
    )
```

```python
import functools
import math

import jax
import jax.numpy as jnp
from jax import lax
from jax.experimental import pallas as pl
from jax.experimental.pallas import tpu as pltpu
from jax.sharding import PartitionSpec as P


SUBSTEPS = 4
MARGIN = 2 * SUBSTEPS

lat_edge = 1.3089969
courant = 0.4
friction = 0.02
rotation = 0.2
frequencies = (0.1405, 0.1454, 0.1379, 0.1458, 0.0729, 0.0676, 0.0725, 0.0649)
diurnal_from = 4

f32 = jnp.float32
bf16 = jnp.bfloat16
LANES = 128


def split_bf16(x):
    high = x.astype(bf16)
    return high, (x - high.astype(f32)).astype(bf16)


def call(kernel, out_shape, in_specs=None, scratch=(), vmem=None):
    params = pltpu.CompilerParams(vmem_limit_bytes=(vmem or 16) << 20)
    kwargs = {} if in_specs is None else {"in_specs": in_specs}
    return pl.pallas_call(
        kernel, out_shape=out_shape, scratch_shapes=scratch, compiler_params=params, **kwargs
    )


def shaped(*dims, dtype=f32):
    return jax.ShapeDtypeStruct(dims, dtype)


def fetch_kernel(first, source, target, turned, sems):
    pieces = sems.shape[0]
    span = target.shape[0] // pieces
    copies = []
    for piece in range(pieces):
        taken = source.at[pl.ds(first + piece * span, span)]
        placed = target.at[pl.ds(piece * span, span)]
        copies.append(pltpu.make_async_copy(taken, placed, sems.at[piece]))
    for copy in copies:
        copy.start()
    for piece, copy in enumerate(copies):
        copy.wait()
        for wave in range(piece * span, (piece + 1) * span):
            turned[wave] = target[wave].T


def pack_kernel(sea, east, north, depth, mask, loading, own, near, away, *rest):
    strips = rest[:-3]
    wet, sems, wet_sem = rest[-3:]
    copies = [pltpu.make_async_copy(mask, wet, wet_sem)]
    for index, ref in ((0, sea), (1, east), (2, north), (3, depth), (5, loading)):
        copies.append(pltpu.make_async_copy(ref, own.at[index], sems.at[index]))
    for copy in copies:
        copy.start()
    odd = (lax.axis_index("lon") & 1) > 0
    lat_index = lax.axis_index("lat")
    rows, lat_dev = sea.shape
    for copy in copies:
        copy.wait()
    filled = wet[...].astype(f32)
    own[4] = filled
    for index in range(rows // MARGIN):
        near[6 + index] = filled[index * MARGIN : (index + 1) * MARGIN]
    for index in range(6):
        cells = own[index]
        first = cells[:MARGIN]
        last = cells[rows - MARGIN :]
        near[index] = jnp.where(odd, first, last)
        away[index] = jnp.where(odd, last, first)
        turned = cells.T
        top = turned[lat_dev - MARGIN :]
        bottom = turned[:MARGIN]
        if len(strips) == 1:
            strips[0][index] = jnp.where(lat_index == 0, top, bottom)
        else:
            strips[0][index] = top
            strips[1][index] = bottom


def turns_trig(turns, total_cols):
    angle = (2.0 * math.pi / total_cols) * (turns % total_cols).astype(f32)
    return jnp.cos(angle), jnp.sin(angle)


def owners(piece, lon_index, gens):
    owner = jnp.zeros(piece.shape, jnp.int32) + lon_index
    for place, gen in enumerate(gens):
        owner = owner ^ (((piece >> (len(gens) - 1 - place)) & 1) * gen)
    return owner


def join_kernel(near, away, *rest):
    sources, targets = rest[: len(rest) // 2], rest[len(rest) // 2 :]
    lat_dev = near.shape[2]
    lane = lax.broadcasted_iota(jnp.int32, (MARGIN, lat_dev), 1)
    edge = jnp.logical_or(lane < MARGIN, lane >= lat_dev - MARGIN)
    for index in range(6):
        corner = jnp.where(edge, near[index], pltpu.roll(away[index], lat_dev // 2, axis=1))
        for source, target in zip(sources, targets):
            target[index] = source[index]
            target[6 + index] = corner


def table_kernel(
    sizes,
    amp_in,
    phase_in,
    love_in,
    counts_in,
    own,
    near,
    forward,
    inverse,
    wet_pair,
    forcing,
    latitude_out,
    love_out,
    counts_out,
    amp,
    phase,
    outer,
    sems,
):
    lon_dev, lat_dev, total_cols, total_rows, wave_dev, gens = sizes
    pairs = ((amp_in, amp), (phase_in, phase), (love_in, love_out), (counts_in, counts_out))
    copies = [
        pltpu.make_async_copy(source, target, sems.at[place])
        for place, (source, target) in enumerate(pairs)
    ]
    for copy in copies:
        copy.start()
    lon_index = lax.axis_index("lon")
    lat_index = lax.axis_index("lat")
    chunk = 2 * wave_dev
    chunks = 1 << len(gens)
    scale = 1.0 / math.sqrt(total_cols)

    def trig(turns):
        return turns_trig(turns, total_cols)

    columns = lon_index * lon_dev + lax.broadcasted_iota(jnp.int32, (wave_dev, lon_dev), 1)
    wave = lax.broadcasted_iota(jnp.int32, (wave_dev, lon_dev), 0)
    cos_in, sin_in = trig(wave * columns)
    cos_in = cos_in * scale
    sin_in = sin_in * scale
    columns = lon_index * lon_dev + lax.broadcasted_iota(jnp.int32, (chunks, lon_dev), 1)
    piece = lax.broadcasted_iota(jnp.int32, (chunks, lon_dev), 0)
    owner = owners(piece, lon_index, gens)
    cos_out, sin_out = trig(owner * wave_dev * columns)
    outer[0] = cos_out
    outer[1] = sin_out
    block = LANES // chunk

    def fill(index, _):
        rows = []
        for inner in range(block):
            at = pl.ds(index * block + inner, 1)
            cos_at, sin_at = outer[0, at], outer[1, at]
            rows.append(cos_at * cos_in - sin_at * sin_in)
            rows.append(-(sin_at * cos_in + cos_at * sin_in))
        rows = jnp.concatenate(rows, axis=0)
        high, low = split_bf16(rows)
        span = pl.ds(pl.multiple_of(index * LANES, LANES), LANES)
        forward[span, :lon_dev] = high
        forward[span, lon_dev:] = low
        high_t, low_t = split_bf16(rows.T)
        inverse[:lon_dev, span] = high_t
        inverse[lon_dev:, span] = low_t
        return 0

    lax.fori_loop(0, chunks // block, fill, 0)
    wet_pair[:lon_dev] = own[4].astype(bf16)
    for index in range(0, lon_dev // MARGIN, 2):
        both = jnp.concatenate([near[6 + index], near[7 + index]], axis=0)
        at = lon_dev + index * MARGIN
        wet_pair[at : at + 2 * MARGIN] = both.astype(bf16)

    wide = lon_dev + 2 * MARGIN
    lane = lax.broadcasted_iota(jnp.int32, (8, 2 * lat_dev), 1)
    row = jnp.where(lane < lat_dev + lat_dev // 2, lane, lane - 2 * lat_dev) + lat_index * lat_dev
    latitude = -lat_edge + 2.0 * lat_edge * (row.astype(f32) + 0.5) / total_rows
    inside = jnp.clip(latitude, -1.5, 1.5)
    cosine = jnp.cos(inside)
    latitude_out[0] = cosine
    latitude_out[1] = 1.0 / cosine
    latitude_out[2] = rotation * jnp.sin(inside)
    semi = jnp.cos(latitude) ** 2
    diurnal = jnp.sin(2.0 * latitude)

    spot = lax.broadcasted_iota(jnp.int32, (8, wide), 1)
    order = 1 + (lax.broadcasted_iota(jnp.int32, (8, wide), 0) & 1)
    spot = jnp.where(spot < lon_dev + MARGIN, spot, spot - wide) + lon_index * lon_dev
    cos_lon, sin_lon = trig(spot * order + total_cols * 2)
    both = jnp.concatenate([cos_lon, sin_lon], axis=0).T
    cos_one, cos_two = both[:, 0:1], both[:, 1:2]
    sin_one, sin_two = both[:, 8:9], both[:, 9:10]

    count = len(frequencies)
    place = lax.broadcasted_iota(jnp.int32, (8, count), 1)
    moment = lax.broadcasted_iota(jnp.int32, (8, count), 0).astype(f32)
    omega = jnp.zeros((8, count), f32)
    for index in range(count):
        omega = jnp.where(place == index, frequencies[index], omega)
    for copy in copies:
        copy.wait()
    argument = omega * moment + phase[...]
    strength = amp[...] * (total_cols / 64.0)
    real = strength * jnp.cos(argument)
    imag = strength * jnp.sin(argument)
    is_semi = place < diurnal_from

    def total(values, chosen):
        return jnp.sum(jnp.where(chosen, values, 0.0), axis=1, keepdims=True)

    semi_real = total(real, is_semi)
    semi_imag = total(imag, is_semi)
    diurnal_real = total(real, jnp.logical_not(is_semi))
    diurnal_imag = total(imag, jnp.logical_not(is_semi))
    for k in range(SUBSTEPS):
        at = slice(k, k + 1)
        along = cos_two * semi_real[at] - sin_two * semi_imag[at]
        across = cos_one * diurnal_real[at] - sin_one * diurnal_imag[at]
        forcing[k] = along * semi[0:1] + across * diurnal[0:1]


def mask_kernel(sizes, pair, far, keep, send):
    lon_dev, total_cols, wave_dev, gens = sizes
    lon_index = lax.axis_index("lon")
    chunks = 1 << (len(gens) - 2)
    scale = 1.0 / math.sqrt(total_cols)
    column = lax.broadcasted_iota(jnp.int32, (wave_dev, lon_dev), 1)
    wave = lax.broadcasted_iota(jnp.int32, (wave_dev, lon_dev), 0)
    spot = lax.broadcasted_iota(jnp.int32, (chunks, lon_dev), 1)
    piece = lax.broadcasted_iota(jnp.int32, (chunks, lon_dev), 0)
    owner = owners(piece, lon_index, gens[2:])
    result = None
    for source, other in ((pair, 0), (far, gens[1])):
        for at, offset in ((0, other), (1, other ^ gens[0])):
            start = (lon_index ^ offset) * lon_dev
            cos_in, sin_in = turns_trig(wave * (column + start), total_cols)
            cos_in = cos_in * scale
            sin_in = sin_in * scale
            cos_out, sin_out = turns_trig(owner * wave_dev * (spot + start), total_cols)
            rows = []
            for index in range(chunks):
                cos_at, sin_at = cos_out[index : index + 1], sin_out[index : index + 1]
                rows.append(cos_at * cos_in - sin_at * sin_in)
                rows.append(-(sin_at * cos_in + cos_at * sin_in))
            high, low = split_bf16(jnp.concatenate(rows, axis=0))
            wet = source[at * lon_dev : (at + 1) * lon_dev]
            term = jnp.dot(
                jnp.concatenate([high, low], axis=1),
                jnp.concatenate([wet, wet], axis=0),
                preferred_element_type=f32,
            )
            result = term if result is None else result + term
    half = keep.shape[0]
    keep[...] = result[:half]
    send[...] = result[half:]


def step_kernel(count, own, near, away, *rest):
    facing = rest[: 1 if count == 2 else 2]
    (
        forcing,
        latitude,
        height_out,
        east_out,
        north_out,
        wet_height,
        wet_sum,
        state,
        static,
    ) = rest[len(facing) :]
    above, below = facing[0], facing[-1]
    lon_dev, lat_dev = own.shape[1:]
    wide = lon_dev + 2 * MARGIN
    lanes = 2 * lat_dev
    lat_index = lax.axis_index("lat")
    odd = (lax.axis_index("lon") & 1) > 0
    has_top = lat_index < count - 1
    has_bottom = lat_index > 0
    middle = jnp.zeros((lat_dev - 2 * MARGIN, lon_dev), f32)
    lane = lax.broadcasted_iota(jnp.int32, (MARGIN, lat_dev), 1)
    at_top = jnp.logical_and(lane < MARGIN, has_top)
    at_bottom = jnp.logical_and(lane >= lat_dev - MARGIN, has_bottom)

    fields = []
    for index in range(6):
        cells = own[index]
        north_rows = jnp.where(has_top, above[index], 0.0)
        south_rows = jnp.where(has_bottom, below[index], 0.0)
        side = jnp.concatenate([north_rows, middle, south_rows], axis=0).T
        corners = []
        for turn in (0, lat_dev // 2):
            north_part, south_part = above[6 + index], below[6 + index]
            if turn:
                north_part = pltpu.roll(north_part, turn, axis=1)
                south_part = pltpu.roll(south_part, turn, axis=1)
            part = jnp.where(at_bottom, south_part, 0.0)
            corners.append(jnp.where(at_top, north_part, part))
        corner_east = jnp.where(odd, corners[1], corners[0])
        corner_west = jnp.where(odd, corners[0], corners[1])
        from_east = jnp.where(odd, away[index], near[index])
        from_west = jnp.where(odd, near[index], away[index])
        left = jnp.concatenate([cells, from_east, from_west], axis=0)
        right = jnp.concatenate([side, corner_east, corner_west], axis=0)
        fields.append(jnp.concatenate([left, right], axis=1))
    for index in range(3):
        state[index] = fields[index]
        static[index] = fields[3 + index]

    def along(f):
        return pltpu.roll(f, wide - 1, axis=0) - pltpu.roll(f, 1, axis=0)

    def across(f):
        return pltpu.roll(f, lanes - 1, axis=1) - pltpu.roll(f, 1, axis=1)

    cosine = latitude[0][0:1]
    secant = latitude[1][0:1]
    coriolis = latitude[2][0:1]

    def substep(k, _):
        east = state[1]
        north = state[2]
        depth = static[0]
        wet = static[1]
        divergence = (along(depth * east) + across(depth * north * cosine)) * 0.5 * secant
        height = state[0] - courant * divergence * wet
        state[0] = height
        pressure = height - forcing[k] - static[2]
        slope_east = along(pressure) * 0.5 * secant
        slope_north = across(pressure) * 0.5
        state[1] = wet * ((1.0 - friction) * east + courant * (coriolis * north - slope_east))
        state[2] = wet * ((1.0 - friction) * north - courant * (coriolis * east + slope_north))
        return 0

    lax.fori_loop(0, SUBSTEPS, substep, 0)
    core = state[0, :lon_dev, :lat_dev]
    height_out[...] = core
    east_out[...] = state[1, :lon_dev, :lat_dev]
    north_out[...] = state[2, :lon_dev, :lat_dev]
    product = core * own[4]
    wet_height[...] = product
    level = jnp.sum(jnp.sum(product, axis=0, keepdims=True), axis=1, keepdims=True)
    wet_sum[...] = jnp.broadcast_to(level, wet_sum.shape)


def fourier_kernel(wet_height, wet_sum, forward, keep, send):
    high, low = split_bf16(wet_height[...])
    top = jnp.concatenate([high, low], axis=1)
    under = jnp.concatenate([high, jnp.zeros_like(low)], axis=1)
    weights = jnp.concatenate([top, under], axis=0)
    half = keep.shape[0]
    cols = wet_height.shape[1]

    def transform(span):
        both = jnp.dot(forward[span], weights, preferred_element_type=f32)
        return both[:, :cols] + both[:, cols:]

    send[:half] = transform(slice(half, 2 * half))
    send[half:] = wet_sum[...]
    keep[...] = transform(slice(0, half))


GROUP = 8


def pair(legendre, wave):
    return jnp.concatenate([legendre[wave], legendre[wave + 1]], axis=1)


def analysis_kernel(first, keep, recv, wet_keep, wet_sum, wet_counts, table, out, *sent):
    lat_dev = keep.shape[1]
    rows = keep.shape[0]
    counts = wet_counts[...].astype(f32)
    total = jnp.sum(jnp.sum(counts, axis=1, keepdims=True), axis=0, keepdims=True)
    mean = wet_sum[0:1, 0:1] / total
    lines = 2 * GROUP
    line = lax.broadcasted_iota(jnp.int32, (lines, lat_dev), 0) & (GROUP - 1)
    for group in range(table.shape[0] // GROUP):
        values = []
        for begin in (first + group * GROUP, rows // 2 + first + group * GROUP):
            span = slice(begin, begin + GROUP)
            wet_span = slice(rows + begin, rows + begin + GROUP)
            values.append((keep[span] + recv[span]) - mean * (wet_keep[span] + recv[wet_span]))
        value = jnp.concatenate(values, axis=0)
        result = None
        for step in range(0, GROUP, 2):
            left = jnp.concatenate(
                [
                    jnp.where(line == step, value, 0.0).astype(bf16),
                    jnp.where(line == step + 1, value, 0.0).astype(bf16),
                ],
                axis=1,
            )
            wave = group * GROUP + step
            right = jnp.concatenate([table[wave], table[wave + 1]], axis=0)
            term = jnp.dot(left, right, preferred_element_type=f32)
            result = term if result is None else result + term
        for target in (out, *sent):
            target[group * lines : (group + 1) * lines] = result.astype(target.dtype)


def synthesis_kernel(sizes, own, recv, love, table, *rest):
    first, wave_dev = sizes
    out = rest[-1]
    lead = rest[:-1]
    lat_dev = out.shape[1]
    lines = 2 * GROUP
    line = lax.broadcasted_iota(jnp.int32, (lines, lat_dev), 0) & (GROUP - 1)
    base = lax.axis_index("lon") * wave_dev + first
    real, imag = [], []
    for group in range(table.shape[0] // GROUP):
        span = slice(group * lines, (group + 1) * lines)
        total = own[span].astype(f32) + recv[span].astype(f32)
        scaled = (love[...] * total).astype(bf16)
        result = None
        for step in range(0, GROUP, 2):
            both = jnp.dot(scaled, pair(table, group * GROUP + step), preferred_element_type=f32)
            left, right = both[:, :lat_dev], both[:, lat_dev:]
            result = left if result is None else jnp.where(line == step, left, result)
            result = jnp.where(line == step + 1, right, result)
        result = jnp.where(base + group * GROUP + line == 0, 1.0, 2.0) * result
        real.append(result[:GROUP])
        imag.append(result[GROUP:])
    if lead:
        half = lead[0].shape[0] // 2
        real.insert(0, lead[0][:half])
        imag.insert(0, lead[0][half:])
    out[...] = jnp.concatenate(real + imag, axis=0).astype(out.dtype)


def inverse_kernel(inverse, near, far, out):
    lon_dev = out.shape[0]
    half = near.shape[0]
    both = jnp.dot(inverse[:, :half], near[...], preferred_element_type=f32)
    both += jnp.dot(inverse[:, half:], far[...], preferred_element_type=f32)
    out[...] = both[:lon_dev] + both[lon_dev:]


def shards(
    sea_level,
    east_velocity,
    north_velocity,
    depth,
    land_mask,
    wet_counts,
    loading_prev,
    tide_amp,
    tide_phase,
    legendre,
    love_factor,
):
    lon_dev, lat_dev = sea_level.shape
    wave_dev, degrees = legendre.shape[:2]
    lon_count = lax.axis_size("lon")
    lat_count = lax.axis_size("lat")
    total_cols = lon_dev * lon_count
    total_rows = lat_dev * lat_count
    bits = lon_count.bit_length() - 1
    lat_bits = lat_count.bit_length() - 1
    assert lon_count == 1 << bits and lat_count == 1 << lat_bits
    gens = [1] + [(1 << b) ^ 1 for b in (1, *range(bits - 1, 1, -1))][: bits - 1]
    vmem = pl.BlockSpec(memory_space=pltpu.VMEM)
    hbm = pl.BlockSpec(memory_space=pltpu.HBM)

    strip = shaped(6, MARGIN, LANES)

    def stay_put(cells):
        return pltpu.with_memory_space_constraint(cells, pltpu.HBM)

    own, near, away, *strips = call(
        pack_kernel,
        [shaped(6, lon_dev, lat_dev), shaped(6 + lon_dev // MARGIN, MARGIN, LANES), strip] + [strip] * (1 if lat_count == 2 else 2),
        in_specs=[hbm] * 6,
        scratch=[
            pltpu.VMEM((lon_dev, lat_dev), jnp.int32),
            pltpu.SemaphoreType.DMA((6,)),
            pltpu.SemaphoreType.DMA,
        ],
    )(*map(stay_put, (sea_level, east_velocity, north_velocity, depth, land_mask, loading_prev)))

    def stay(b):
        return b

    def nearby(b):
        return b ^ 1

    def beyond(b):
        return (b + 1 if b & 1 else b - 1) % lon_count

    def shift(cells, lat_step, move):
        pairs = []
        for a in range(lat_count):
            target = a ^ 1 if lat_step is None else a + lat_step
            if 0 <= target < lat_count:
                for b in range(lon_count):
                    pairs.append((a * lon_count + b, target * lon_count + move(b)))
        return lax.ppermute(cells, ("lat", "lon"), pairs)

    away = shift(away, 0, beyond)
    near = shift(near, 0, nearby)

    chunk = 2 * wave_dev
    lines = chunk * lon_count
    half = lines // 2
    wide = lon_dev + 2 * MARGIN
    forward, inverse, wet_pair, forcing, latitude, love, counts = call(
        functools.partial(
            table_kernel, (lon_dev, lat_dev, total_cols, total_rows, wave_dev, tuple(gens))
        ),
        [
            shaped(lines, 2 * lon_dev, dtype=bf16),
            shaped(2 * lon_dev, lines, dtype=bf16),
            shaped(2 * lon_dev, lat_dev, dtype=bf16),
            shaped(SUBSTEPS, wide, 2 * lat_dev),
            shaped(3, 8, 2 * lat_dev),
            shaped(1, degrees),
            shaped(*wet_counts.shape, dtype=jnp.int32),
        ],
        in_specs=[hbm] * 4 + [vmem] * 2,
        scratch=[
            pltpu.VMEM((1, len(frequencies)), f32),
            pltpu.VMEM((1, len(frequencies)), f32),
            pltpu.VMEM((2, lon_count, lon_dev), f32),
            pltpu.SemaphoreType.DMA((4,)),
        ],
    )(
        stay_put(tide_amp[None]),
        stay_put(tide_phase[None]),
        stay_put(love_factor[None]),
        stay_put(wet_counts),
        own,
        near,
    )

    def swap(cells, gen):
        return lax.ppermute(cells, "lon", [(i, i ^ gen) for i in range(lon_count)])

    wet_far = swap(wet_pair, gens[1])

    strips = call(join_kernel, [shaped(12, MARGIN, LANES)] * len(strips))(near, away, *strips)
    if lat_count == 2:
        facing = [shift(strips[0], None, stay)]
    else:
        facing = [shift(strips[1], -1, stay), shift(strips[0], 1, stay)]
    height, east_new, north_new, wet_height, wet_sum = call(
        functools.partial(step_kernel, lat_count),
        [shaped(lon_dev, lat_dev)] * 4 + [shaped(8, lat_dev)],
        in_specs=[vmem] * (5 + len(facing)),
        scratch=[pltpu.VMEM((3, wide, 2 * lat_dev), f32)] * 2,
    )(own, near, away, *facing, forcing, latitude)

    keep, send = call(
        fourier_kernel, [shaped(half, lat_dev), shaped(half + 8, lat_dev)]
    )(wet_height, wet_sum, forward)
    recv = swap(send, gens[0])
    wet_keep, wet_send = call(
        functools.partial(mask_kernel, (lon_dev, total_cols, wave_dev, tuple(gens))),
        [shaped(half // 4, lat_dev)] * 2,
    )(wet_pair, wet_far)
    wet_recv = swap(wet_send, gens[2])
    level = wet_sum + recv[half:]
    joined = lat_count == 2
    part = half // 2
    send = jnp.concatenate([keep[part:] + recv[part:half], level], axis=0)
    keep = keep[:part] + recv[:part]
    recv = swap(send, gens[1])
    arrived = recv[part:]
    if joined:
        arrived = arrived + shift(level, None, nearby)
        arrived = arrived + shift(level, None, lambda b: b ^ gens[1])
    level = level + arrived
    for place, gen in enumerate(gens[2:]):
        part = keep.shape[0] // 2
        sends = [keep[part:] + recv[part : 2 * part]]
        keep = keep[:part] + recv[:part]
        if place > 0:
            sends.append(wet_keep[part:] + wet_recv[part : 2 * part])
            wet_keep = wet_keep[:part] + wet_recv[:part]
        recv = swap(jnp.concatenate([*sends, level], axis=0), gen)
        if place > 0:
            wet_recv = recv[part : 2 * part]
            level = level + recv[2 * part :]
        else:
            level = level + recv[part:]
    if not joined:
        for b in range(lat_bits):
            level = level + lax.ppermute(
                level, "lat", [(i, i ^ (1 << b)) for i in range(lat_count)]
            )

    parts = 2
    waves = wave_dev // parts
    tables = []
    for piece in range(parts):
        tables.append(
            call(
                functools.partial(fetch_kernel, piece * waves),
                [
                    pltpu.VMEM((waves, degrees, lat_dev), bf16),
                    pltpu.VMEM((waves, lat_dev, degrees), bf16),
                ],
                in_specs=[hbm],
                scratch=[pltpu.SemaphoreType.DMA((4,))],
            )(stay_put(legendre))
        )
    sums = []
    for piece in range(parts):
        mine, moving = call(
            functools.partial(analysis_kernel, piece * waves),
            [shaped(2 * waves, degrees), shaped(2 * waves, degrees, dtype=bf16)],
            in_specs=[vmem] * 6,
        )(keep, recv, wet_keep, level, counts, tables[piece][1])
        for b in range(lat_bits):
            other = lax.ppermute(moving, "lat", [(i, i ^ (1 << b)) for i in range(lat_count)])
            if b < lat_bits - 1:
                mine = mine + other.astype(f32)
                moving = mine.astype(bf16)
        sums.append((mine, other))
    spectra = ()
    for piece in range(parts):
        last = piece == parts - 1
        spectra = (
            call(
                functools.partial(synthesis_kernel, (piece * waves, wave_dev)),
                shaped(2 * waves * (piece + 1), lat_dev, dtype=bf16 if last else f32),
                in_specs=[vmem] * (4 + len(spectra)),
            )(*sums[piece], love, tables[piece][0], *spectra),
        )
    near = spectra[0]
    for gen in gens[:0:-1]:
        near = jnp.concatenate([near, swap(near, gen)], axis=0)
    far = swap(near, gens[0])
    loading_new = call(inverse_kernel, shaped(lon_dev, lat_dev))(inverse, near, far)
    return (height, east_new, north_new, loading_new)


def solution(mesh):
    tile = P("lon", "lat")
    return jax.shard_map(
        shards,
        mesh=mesh,
        in_specs=(tile,) * 5 + (P(), tile, P(), P(), P("lon", None, "lat"), P()),
        out_specs=(tile,) * 4,
        check_vma=False,
    )
```

```python
import functools
import math

import jax
import jax.numpy as jnp
from jax import lax
from jax.experimental import pallas as pl
from jax.experimental.pallas import tpu as pltpu
from jax.sharding import PartitionSpec as P


SUBSTEPS = 4
MARGIN = 2 * SUBSTEPS

lat_edge = 1.3089969
courant = 0.4
friction = 0.02
rotation = 0.2
frequencies = (0.1405, 0.1454, 0.1379, 0.1458, 0.0729, 0.0676, 0.0725, 0.0649)
diurnal_from = 4

f32 = jnp.float32
bf16 = jnp.bfloat16
LANES = 128


def split_bf16(x):
    high = x.astype(bf16)
    return high, (x - high.astype(f32)).astype(bf16)


def call(kernel, out_shape, in_specs=None, scratch=(), vmem=None):
    params = pltpu.CompilerParams(vmem_limit_bytes=(vmem or 16) << 20)
    kwargs = {} if in_specs is None else {"in_specs": in_specs}
    return pl.pallas_call(
        kernel, out_shape=out_shape, scratch_shapes=scratch, compiler_params=params, **kwargs
    )


def shaped(*dims, dtype=f32):
    return jax.ShapeDtypeStruct(dims, dtype)


def fetch_kernel(first, source, target, turned, sems):
    pieces = sems.shape[0]
    span = target.shape[0] // pieces
    copies = []
    for piece in range(pieces):
        taken = source.at[pl.ds(first + piece * span, span)]
        placed = target.at[pl.ds(piece * span, span)]
        copies.append(pltpu.make_async_copy(taken, placed, sems.at[piece]))
    for copy in copies:
        copy.start()
    for piece, copy in enumerate(copies):
        copy.wait()
        for wave in range(piece * span, (piece + 1) * span):
            turned[wave] = target[wave].T


def strip_kernel(sea, east, north, depth, mask, loading, near, away, wet, sems):
    odd = lax.axis_index("lon") & 1
    rows = sea.shape[0]
    copies = [pltpu.make_async_copy(mask, wet, sems.at[0, 4])]
    for side, target in enumerate((near, away)):
        start = (1 - odd if side == 0 else odd) * (rows - MARGIN)
        span = pl.ds(pl.multiple_of(start, MARGIN), MARGIN)
        for index, source in ((0, sea), (1, east), (2, north), (3, depth), (5, loading)):
            copies.append(
                pltpu.make_async_copy(source.at[span], target.at[index], sems.at[side, index])
            )
    for copy in copies:
        copy.start()
    for copy in copies:
        copy.wait()
    for index in range(rows // MARGIN):
        near[6 + index] = wet[index * MARGIN : (index + 1) * MARGIN].astype(f32)
    first = near[6]
    last = near[5 + rows // MARGIN]
    near[4] = jnp.where(odd > 0, first, last)
    away[4] = jnp.where(odd > 0, last, first)


def pack_kernel(sea, east, north, depth, mask, loading, own, *rest):
    strips = rest[:-3]
    wet, sems, wet_sem = rest[-3:]
    copies = [pltpu.make_async_copy(mask, wet, wet_sem)]
    for index, ref in ((0, sea), (1, east), (2, north), (3, depth), (5, loading)):
        copies.append(pltpu.make_async_copy(ref, own.at[index], sems.at[index]))
    for copy in copies:
        copy.start()
    lat_index = lax.axis_index("lat")
    lat_dev = sea.shape[1]
    for copy in copies:
        copy.wait()
    own[4] = wet[...].astype(f32)
    for index in range(6):
        turned = own[index].T
        top = turned[lat_dev - MARGIN :]
        bottom = turned[:MARGIN]
        if len(strips) == 1:
            strips[0][index] = jnp.where(lat_index == 0, top, bottom)
        else:
            strips[0][index] = top
            strips[1][index] = bottom


def turns_trig(turns, total_cols):
    angle = (2.0 * math.pi / total_cols) * (turns % total_cols).astype(f32)
    return jnp.cos(angle), jnp.sin(angle)


def owners(piece, lon_index, gens):
    owner = jnp.zeros(piece.shape, jnp.int32) + lon_index
    for place, gen in enumerate(gens):
        owner = owner ^ (((piece >> (len(gens) - 1 - place)) & 1) * gen)
    return owner


def join_kernel(own, near, away, *rest):
    count = len(rest) // 2
    sources, targets, wet_pair = rest[:count], rest[count:-1], rest[-1]
    lon_dev, lat_dev = own.shape[1:]
    wet_pair[:lon_dev] = own[4].astype(bf16)
    for index in range(0, lon_dev // MARGIN, 2):
        both = jnp.concatenate([near[6 + index], near[7 + index]], axis=0)
        at = lon_dev + index * MARGIN
        wet_pair[at : at + 2 * MARGIN] = both.astype(bf16)
    lane = lax.broadcasted_iota(jnp.int32, (MARGIN, lat_dev), 1)
    edge = jnp.logical_or(lane < MARGIN, lane >= lat_dev - MARGIN)
    for index in range(6):
        corner = jnp.where(edge, near[index], pltpu.roll(away[index], lat_dev // 2, axis=1))
        for source, target in zip(sources, targets):
            target[index] = source[index]
            target[6 + index] = corner


def table_kernel(
    sizes,
    amp_in,
    phase_in,
    love_in,
    counts_in,
    forward,
    inverse,
    forcing,
    latitude_out,
    love_out,
    counts_out,
    amp,
    phase,
    outer,
    sems,
):
    lon_dev, lat_dev, total_cols, total_rows, wave_dev, gens = sizes
    pairs = ((amp_in, amp), (phase_in, phase), (love_in, love_out), (counts_in, counts_out))
    copies = [
        pltpu.make_async_copy(source, target, sems.at[place])
        for place, (source, target) in enumerate(pairs)
    ]
    for copy in copies:
        copy.start()
    lon_index = lax.axis_index("lon")
    lat_index = lax.axis_index("lat")
    chunk = 2 * wave_dev
    chunks = 1 << len(gens)
    scale = 1.0 / math.sqrt(total_cols)

    def trig(turns):
        return turns_trig(turns, total_cols)

    columns = lon_index * lon_dev + lax.broadcasted_iota(jnp.int32, (wave_dev, lon_dev), 1)
    wave = lax.broadcasted_iota(jnp.int32, (wave_dev, lon_dev), 0)
    cos_in, sin_in = trig(wave * columns)
    cos_in = cos_in * scale
    sin_in = sin_in * scale
    columns = lon_index * lon_dev + lax.broadcasted_iota(jnp.int32, (chunks, lon_dev), 1)
    piece = lax.broadcasted_iota(jnp.int32, (chunks, lon_dev), 0)
    owner = owners(piece, lon_index, gens)
    cos_out, sin_out = trig(owner * wave_dev * columns)
    outer[0] = cos_out
    outer[1] = sin_out
    block = LANES // chunk

    def fill(index, _):
        rows = []
        for inner in range(block):
            at = pl.ds(index * block + inner, 1)
            cos_at, sin_at = outer[0, at], outer[1, at]
            rows.append(cos_at * cos_in - sin_at * sin_in)
            rows.append(-(sin_at * cos_in + cos_at * sin_in))
        rows = jnp.concatenate(rows, axis=0)
        high, low = split_bf16(rows)
        span = pl.ds(pl.multiple_of(index * LANES, LANES), LANES)
        forward[span, :lon_dev] = high
        forward[span, lon_dev:] = low
        high_t, low_t = split_bf16(rows.T)
        inverse[:lon_dev, span] = high_t
        inverse[lon_dev:, span] = low_t
        return 0

    lax.fori_loop(0, chunks // block, fill, 0)
    wide = lon_dev + 2 * MARGIN
    lane = lax.broadcasted_iota(jnp.int32, (8, 2 * lat_dev), 1)
    row = jnp.where(lane < lat_dev + lat_dev // 2, lane, lane - 2 * lat_dev) + lat_index * lat_dev
    latitude = -lat_edge + 2.0 * lat_edge * (row.astype(f32) + 0.5) / total_rows
    inside = jnp.clip(latitude, -1.5, 1.5)
    cosine = jnp.cos(inside)
    latitude_out[0] = cosine
    latitude_out[1] = 1.0 / cosine
    latitude_out[2] = rotation * jnp.sin(inside)
    semi = jnp.cos(latitude) ** 2
    diurnal = jnp.sin(2.0 * latitude)

    spot = lax.broadcasted_iota(jnp.int32, (8, wide), 1)
    order = 1 + (lax.broadcasted_iota(jnp.int32, (8, wide), 0) & 1)
    spot = jnp.where(spot < lon_dev + MARGIN, spot, spot - wide) + lon_index * lon_dev
    cos_lon, sin_lon = trig(spot * order + total_cols * 2)
    both = jnp.concatenate([cos_lon, sin_lon], axis=0).T
    cos_one, cos_two = both[:, 0:1], both[:, 1:2]
    sin_one, sin_two = both[:, 8:9], both[:, 9:10]

    count = len(frequencies)
    place = lax.broadcasted_iota(jnp.int32, (8, count), 1)
    moment = lax.broadcasted_iota(jnp.int32, (8, count), 0).astype(f32)
    omega = jnp.zeros((8, count), f32)
    for index in range(count):
        omega = jnp.where(place == index, frequencies[index], omega)
    for copy in copies:
        copy.wait()
    argument = omega * moment + phase[...]
    strength = amp[...] * (total_cols / 64.0)
    real = strength * jnp.cos(argument)
    imag = strength * jnp.sin(argument)
    is_semi = place < diurnal_from

    def total(values, chosen):
        return jnp.sum(jnp.where(chosen, values, 0.0), axis=1, keepdims=True)

    semi_real = total(real, is_semi)
    semi_imag = total(imag, is_semi)
    diurnal_real = total(real, jnp.logical_not(is_semi))
    diurnal_imag = total(imag, jnp.logical_not(is_semi))
    for k in range(SUBSTEPS):
        at = slice(k, k + 1)
        along = cos_two * semi_real[at] - sin_two * semi_imag[at]
        across = cos_one * diurnal_real[at] - sin_one * diurnal_imag[at]
        forcing[k] = along * semi[0:1] + across * diurnal[0:1]


def mask_kernel(sizes, pair, far, keep, send):
    lon_dev, total_cols, wave_dev, gens = sizes
    lon_index = lax.axis_index("lon")
    chunks = 1 << (len(gens) - 2)
    scale = 1.0 / math.sqrt(total_cols)
    column = lax.broadcasted_iota(jnp.int32, (wave_dev, lon_dev), 1)
    wave = lax.broadcasted_iota(jnp.int32, (wave_dev, lon_dev), 0)
    spot = lax.broadcasted_iota(jnp.int32, (chunks, lon_dev), 1)
    piece = lax.broadcasted_iota(jnp.int32, (chunks, lon_dev), 0)
    owner = owners(piece, lon_index, gens[2:])
    result = None
    for source, other in ((pair, 0), (far, gens[1])):
        for at, offset in ((0, other), (1, other ^ gens[0])):
            start = (lon_index ^ offset) * lon_dev
            cos_in, sin_in = turns_trig(wave * (column + start), total_cols)
            cos_in = cos_in * scale
            sin_in = sin_in * scale
            cos_out, sin_out = turns_trig(owner * wave_dev * (spot + start), total_cols)
            rows = []
            for index in range(chunks):
                cos_at, sin_at = cos_out[index : index + 1], sin_out[index : index + 1]
                rows.append(cos_at * cos_in - sin_at * sin_in)
                rows.append(-(sin_at * cos_in + cos_at * sin_in))
            high, low = split_bf16(jnp.concatenate(rows, axis=0))
            wet = source[at * lon_dev : (at + 1) * lon_dev]
            term = jnp.dot(
                jnp.concatenate([high, low], axis=1),
                jnp.concatenate([wet, wet], axis=0),
                preferred_element_type=f32,
            )
            result = term if result is None else result + term
    half = keep.shape[0]
    keep[...] = result[:half]
    send[...] = result[half:]


def along(f):
    return pltpu.roll(f, f.shape[0] - 1, axis=0) - pltpu.roll(f, 1, axis=0)


def across(f):
    return pltpu.roll(f, f.shape[1] - 1, axis=1) - pltpu.roll(f, 1, axis=1)


def rise(state, static, rows):
    cosine, secant, _ = rows
    depth = static[0]
    divergence = (along(depth * state[1]) + across(depth * state[2] * cosine)) * 0.5 * secant
    state[0] = state[0] - courant * divergence * static[1]


def veer(state, static, forcing, rows):
    _, secant, coriolis = rows
    east = state[1]
    north = state[2]
    wet = static[1]
    pressure = state[0] - forcing - static[2]
    slope_east = along(pressure) * 0.5 * secant
    slope_north = across(pressure) * 0.5
    return (
        wet * ((1.0 - friction) * east + courant * (coriolis * north - slope_east)),
        wet * ((1.0 - friction) * north - courant * (coriolis * east + slope_north)),
    )


def step_kernel(count, own, near, away, *rest):
    facing = rest[: 1 if count == 2 else 2]
    (
        forcing,
        latitude,
        forward,
        keep,
        send,
        wet_sum,
        state,
        static,
    ) = rest[len(facing) :]
    above, below = facing[0], facing[-1]
    lon_dev, lat_dev = own.shape[1:]
    lat_index = lax.axis_index("lat")
    odd = (lax.axis_index("lon") & 1) > 0
    has_top = lat_index < count - 1
    has_bottom = lat_index > 0
    middle = jnp.zeros((lat_dev - 2 * MARGIN, lon_dev), f32)
    lane = lax.broadcasted_iota(jnp.int32, (MARGIN, lat_dev), 1)
    at_top = jnp.logical_and(lane < MARGIN, has_top)
    at_bottom = jnp.logical_and(lane >= lat_dev - MARGIN, has_bottom)

    fields = []
    for index in range(6):
        cells = own[index]
        north_rows = jnp.where(has_top, above[index], 0.0)
        south_rows = jnp.where(has_bottom, below[index], 0.0)
        side = jnp.concatenate([north_rows, middle, south_rows], axis=0).T
        corners = []
        for turn in (0, lat_dev // 2):
            north_part, south_part = above[6 + index], below[6 + index]
            if turn:
                north_part = pltpu.roll(north_part, turn, axis=1)
                south_part = pltpu.roll(south_part, turn, axis=1)
            part = jnp.where(at_bottom, south_part, 0.0)
            corners.append(jnp.where(at_top, north_part, part))
        corner_east = jnp.where(odd, corners[1], corners[0])
        corner_west = jnp.where(odd, corners[0], corners[1])
        from_east = jnp.where(odd, away[index], near[index])
        from_west = jnp.where(odd, near[index], away[index])
        left = jnp.concatenate([cells, from_east, from_west], axis=0)
        right = jnp.concatenate([side, corner_east, corner_west], axis=0)
        fields.append(jnp.concatenate([left, right], axis=1))
    for index in range(3):
        state[index] = fields[index]
        static[index] = fields[3 + index]

    rows = tuple(latitude[index][0:1] for index in range(3))

    def substep(k, _):
        rise(state, static, rows)
        state[1], state[2] = veer(state, static, forcing[k], rows)
        return 0

    lax.fori_loop(0, SUBSTEPS - 1, substep, 0)
    rise(state, static, rows)
    product = state[0, :lon_dev, :lat_dev] * own[4]
    level = jnp.sum(jnp.sum(product, axis=0, keepdims=True), axis=1, keepdims=True)
    level = jnp.broadcast_to(level, wet_sum.shape)
    wet_sum[...] = level
    high, low = split_bf16(product)
    upper = jnp.concatenate([high, low], axis=1)
    under = jnp.concatenate([high, jnp.zeros_like(low)], axis=1)
    weights = jnp.concatenate([upper, under], axis=0)
    half = keep.shape[0]

    def transform(span):
        both = jnp.dot(forward[span], weights, preferred_element_type=f32)
        return both[:, :lat_dev] + both[:, lat_dev:]

    send[:half] = transform(slice(half, 2 * half))
    send[half:] = level
    keep[...] = transform(slice(0, half))


def finish_kernel(state, static, forcing, latitude, height_out, east_out, north_out):
    lon_dev, lat_dev = height_out.shape
    rows = tuple(latitude[index][0:1] for index in range(3))
    east, north = veer(state, static, forcing[SUBSTEPS - 1], rows)
    height_out[...] = state[0, :lon_dev, :lat_dev]
    east_out[...] = east[:lon_dev, :lat_dev]
    north_out[...] = north[:lon_dev, :lat_dev]


GROUP = 8


def pair(legendre, wave):
    return jnp.concatenate([legendre[wave], legendre[wave + 1]], axis=1)


def locate(table, second, wave):
    held = table.shape[0]
    return (table, wave) if wave < held else (second, wave - held)


def analysis_kernel(sizes, keep, recv, wet_keep, wet_sum, wet_counts, table, second, *outs):
    first, waves = sizes
    lat_dev = keep.shape[1]
    rows = keep.shape[0]
    counts = wet_counts[...].astype(f32)
    total = jnp.sum(jnp.sum(counts, axis=1, keepdims=True), axis=0, keepdims=True)
    mean = wet_sum[0:1, 0:1] / total
    lines = 2 * GROUP
    line = lax.broadcasted_iota(jnp.int32, (lines, lat_dev), 0) & (GROUP - 1)
    for group in range(waves // GROUP):
        values = []
        for begin in (first + group * GROUP, rows // 2 + first + group * GROUP):
            span = slice(begin, begin + GROUP)
            wet_span = slice(rows + begin, rows + begin + GROUP)
            values.append((keep[span] + recv[span]) - mean * (wet_keep[span] + recv[wet_span]))
        value = jnp.concatenate(values, axis=0)
        result = None
        for step in range(0, GROUP, 2):
            left = jnp.concatenate(
                [
                    jnp.where(line == step, value, 0.0).astype(bf16),
                    jnp.where(line == step + 1, value, 0.0).astype(bf16),
                ],
                axis=1,
            )
            source, wave = locate(table, second, first + group * GROUP + step)
            right = jnp.concatenate([source[wave], source[wave + 1]], axis=0)
            term = jnp.dot(left, right, preferred_element_type=f32)
            result = term if result is None else result + term
        for target in outs:
            target[group * lines : (group + 1) * lines] = result.astype(target.dtype)


def synthesis_kernel(sizes, own, recv, love, table, second, *rest):
    first, waves, wave_dev = sizes
    out = rest[-1]
    lead = rest[:-1]
    lat_dev = out.shape[1]
    lines = 2 * GROUP
    line = lax.broadcasted_iota(jnp.int32, (lines, lat_dev), 0) & (GROUP - 1)
    base = lax.axis_index("lon") * wave_dev + first
    real, imag = [], []
    for group in range(waves // GROUP):
        span = slice(group * lines, (group + 1) * lines)
        total = own[span].astype(f32) + recv[span].astype(f32)
        scaled = (love[...] * total).astype(bf16)
        result = None
        for step in range(0, GROUP, 2):
            source, wave = locate(table, second, first + group * GROUP + step)
            both = jnp.dot(scaled, pair(source, wave), preferred_element_type=f32)
            left, right = both[:, :lat_dev], both[:, lat_dev:]
            result = left if result is None else jnp.where(line == step, left, result)
            result = jnp.where(line == step + 1, right, result)
        result = jnp.where(base + group * GROUP + line == 0, 1.0, 2.0) * result
        real.append(result[:GROUP])
        imag.append(result[GROUP:])
    if lead:
        half = lead[0].shape[0] // 2
        real.insert(0, lead[0][:half])
        imag.insert(0, lead[0][half:])
    out[...] = jnp.concatenate(real + imag, axis=0).astype(out.dtype)


def inverse_near_kernel(inverse, near, out):
    half = near.shape[0]
    out[...] = jnp.dot(inverse[:, :half], near[...], preferred_element_type=f32)


def inverse_far_kernel(inverse, started, far, out):
    lon_dev = out.shape[0]
    half = far.shape[0]
    both = started[...] + jnp.dot(inverse[:, half:], far[...], preferred_element_type=f32)
    out[...] = both[:lon_dev] + both[lon_dev:]


def shards(
    sea_level,
    east_velocity,
    north_velocity,
    depth,
    land_mask,
    wet_counts,
    loading_prev,
    tide_amp,
    tide_phase,
    legendre,
    love_factor,
):
    lon_dev, lat_dev = sea_level.shape
    wave_dev, degrees = legendre.shape[:2]
    lon_count = lax.axis_size("lon")
    lat_count = lax.axis_size("lat")
    total_cols = lon_dev * lon_count
    total_rows = lat_dev * lat_count
    bits = lon_count.bit_length() - 1
    lat_bits = lat_count.bit_length() - 1
    assert lon_count == 1 << bits and lat_count == 1 << lat_bits
    gens = [1] + [(1 << b) ^ 1 for b in (1, *range(bits - 1, 1, -1))][: bits - 1]
    vmem = pl.BlockSpec(memory_space=pltpu.VMEM)
    hbm = pl.BlockSpec(memory_space=pltpu.HBM)

    strip = shaped(6, MARGIN, LANES)

    def stay_put(cells):
        return pltpu.with_memory_space_constraint(cells, pltpu.HBM)

    fields = tuple(
        map(stay_put, (sea_level, east_velocity, north_velocity, depth, land_mask, loading_prev))
    )
    near, away = call(
        strip_kernel,
        [shaped(6 + lon_dev // MARGIN, MARGIN, LANES), strip],
        in_specs=[hbm] * 6,
        scratch=[
            pltpu.VMEM((lon_dev, lat_dev), jnp.int32),
            pltpu.SemaphoreType.DMA((2, 6)),
        ],
    )(*fields)
    own, *strips = call(
        pack_kernel,
        [shaped(6, lon_dev, lat_dev)] + [strip] * (1 if lat_count == 2 else 2),
        in_specs=[hbm] * 6,
        scratch=[
            pltpu.VMEM((lon_dev, lat_dev), jnp.int32),
            pltpu.SemaphoreType.DMA((6,)),
            pltpu.SemaphoreType.DMA,
        ],
    )(*fields)

    def stay(b):
        return b

    def nearby(b):
        return b ^ 1

    def beyond(b):
        return (b + 1 if b & 1 else b - 1) % lon_count

    def shift(cells, lat_step, move):
        pairs = []
        for a in range(lat_count):
            target = a ^ 1 if lat_step is None else a + lat_step
            if 0 <= target < lat_count:
                for b in range(lon_count):
                    pairs.append((a * lon_count + b, target * lon_count + move(b)))
        return lax.ppermute(cells, ("lat", "lon"), pairs)

    away = shift(away, 0, beyond)
    near = shift(near, 0, nearby)

    *strips, wet_pair = call(
        join_kernel,
        [shaped(12, MARGIN, LANES)] * len(strips)
        + [shaped(2 * lon_dev, lat_dev, dtype=bf16)],
    )(own, near, away, *strips)
    if lat_count == 2:
        facing = [shift(strips[0], None, stay)]
    else:
        facing = [shift(strips[1], -1, stay), shift(strips[0], 1, stay)]
    chunk = 2 * wave_dev
    lines = chunk * lon_count
    half = lines // 2
    wide = lon_dev + 2 * MARGIN
    forward, inverse, forcing, latitude, love, counts = call(
        functools.partial(
            table_kernel, (lon_dev, lat_dev, total_cols, total_rows, wave_dev, tuple(gens))
        ),
        [
            shaped(lines, 2 * lon_dev, dtype=bf16),
            shaped(2 * lon_dev, lines, dtype=bf16),
            shaped(SUBSTEPS, wide, 2 * lat_dev),
            shaped(3, 8, 2 * lat_dev),
            shaped(1, degrees),
            shaped(*wet_counts.shape, dtype=jnp.int32),
        ],
        in_specs=[hbm] * 4,
        scratch=[
            pltpu.VMEM((1, len(frequencies)), f32),
            pltpu.VMEM((1, len(frequencies)), f32),
            pltpu.VMEM((2, lon_count, lon_dev), f32),
            pltpu.SemaphoreType.DMA((4,)),
        ],
    )(
        stay_put(tide_amp[None]),
        stay_put(tide_phase[None]),
        stay_put(love_factor[None]),
        stay_put(wet_counts),
    )

    def swap(cells, gen):
        return lax.ppermute(cells, "lon", [(i, i ^ gen) for i in range(lon_count)])

    wet_far = swap(wet_pair, gens[1])

    keep, send, wet_sum, state, static = call(
        functools.partial(step_kernel, lat_count),
        [shaped(half, lat_dev), shaped(half + 8, lat_dev), shaped(8, lat_dev)]
        + [pltpu.VMEM((3, wide, 2 * lat_dev), f32)] * 2,
        in_specs=[vmem] * (6 + len(facing)),
    )(own, near, away, *facing, forcing, latitude, forward)

    recv = swap(send, gens[0])
    wet_keep, wet_send = call(
        functools.partial(mask_kernel, (lon_dev, total_cols, wave_dev, tuple(gens))),
        [shaped(half // 4, lat_dev)] * 2,
    )(wet_pair, wet_far)
    wet_recv = swap(wet_send, gens[2])
    level = wet_sum + recv[half:]
    joined = lat_count == 2
    part = half // 2
    send = jnp.concatenate([keep[part:] + recv[part:half], level], axis=0)
    keep = keep[:part] + recv[:part]
    recv = swap(send, gens[1])
    arrived = recv[part:]
    if joined:
        arrived = arrived + shift(level, None, nearby)
        arrived = arrived + shift(level, None, lambda b: b ^ gens[1])
    level = level + arrived
    for place, gen in enumerate(gens[2:]):
        part = keep.shape[0] // 2
        sends = [keep[part:] + recv[part : 2 * part]]
        keep = keep[:part] + recv[:part]
        if place > 0:
            sends.append(wet_keep[part:] + wet_recv[part : 2 * part])
            wet_keep = wet_keep[:part] + wet_recv[:part]
        recv = swap(jnp.concatenate([*sends, level], axis=0), gen)
        if place > 0:
            wet_recv = recv[part : 2 * part]
            level = level + recv[2 * part :]
        else:
            level = level + recv[part:]
    if not joined:
        for b in range(lat_bits):
            level = level + lax.ppermute(
                level, "lat", [(i, i ^ (1 << b)) for i in range(lat_count)]
            )

    parts = 2
    waves = wave_dev // parts
    tables = []
    for piece in range(parts):
        tables.append(
            call(
                functools.partial(fetch_kernel, piece * waves),
                [
                    pltpu.VMEM((waves, degrees, lat_dev), bf16),
                    pltpu.VMEM((waves, lat_dev, degrees), bf16),
                ],
                in_specs=[hbm],
                scratch=[pltpu.SemaphoreType.DMA((4,))],
            )(stay_put(legendre))
        )
    turned = [table[1] for table in tables]
    tables = [table[0] for table in tables]
    pieces = ((0, wave_dev - wave_dev // 4), (wave_dev - wave_dev // 4, wave_dev // 4))
    sums = []
    for first, waves in pieces:
        mine, moving = call(
            functools.partial(analysis_kernel, (first, waves)),
            [shaped(2 * waves, degrees), shaped(2 * waves, degrees, dtype=bf16)],
            in_specs=[vmem] * 7,
        )(keep, recv, wet_keep, level, counts, *turned)
        for b in range(lat_bits):
            other = lax.ppermute(moving, "lat", [(i, i ^ (1 << b)) for i in range(lat_count)])
            if b < lat_bits - 1:
                mine = mine + other.astype(f32)
                moving = mine.astype(bf16)
        sums.append((mine, other))
    spectra = ()
    for piece, (first, waves) in enumerate(pieces):
        last = piece == len(pieces) - 1
        spectra = (
            call(
                functools.partial(synthesis_kernel, (first, waves, wave_dev)),
                shaped(2 * (first + waves), lat_dev, dtype=bf16 if last else f32),
                in_specs=[vmem] * (5 + len(spectra)),
            )(*sums[piece], love, *tables, *spectra),
        )
    near = spectra[0]
    for gen in gens[:0:-1]:
        near = jnp.concatenate([near, swap(near, gen)], axis=0)
    far = swap(near, gens[0])
    started = call(inverse_near_kernel, shaped(2 * lon_dev, lat_dev))(inverse, near)
    loading_new = call(inverse_far_kernel, shaped(lon_dev, lat_dev))(inverse, started, far)
    height, east_new, north_new = call(finish_kernel, [shaped(lon_dev, lat_dev)] * 3)(
        state, static, forcing, latitude
    )
    return (height, east_new, north_new, loading_new)


def solution(mesh):
    tile = P("lon", "lat")
    return jax.shard_map(
        shards,
        mesh=mesh,
        in_specs=(tile,) * 5 + (P(), tile, P(), P(), P("lon", None, "lat"), P()),
        out_specs=(tile,) * 4,
        check_vma=False,
    )
```

```python
import functools
import math

import jax
import jax.numpy as jnp
from jax import lax
from jax.experimental import pallas as pl
from jax.experimental.pallas import tpu as pltpu
from jax.sharding import PartitionSpec as P


SUBSTEPS = 4
MARGIN = 2 * SUBSTEPS

lat_edge = 1.3089969
courant = 0.4
friction = 0.02
rotation = 0.2
frequencies = (0.1405, 0.1454, 0.1379, 0.1458, 0.0729, 0.0676, 0.0725, 0.0649)
diurnal_from = 4

f32 = jnp.float32
bf16 = jnp.bfloat16
LANES = 128


def split_bf16(x):
    high = x.astype(bf16)
    return high, (x - high.astype(f32)).astype(bf16)


def call(kernel, out_shape, in_specs=None, scratch=(), vmem=None):
    params = pltpu.CompilerParams(vmem_limit_bytes=(vmem or 16) << 20)
    kwargs = {} if in_specs is None else {"in_specs": in_specs}
    return pl.pallas_call(
        kernel, out_shape=out_shape, scratch_shapes=scratch, compiler_params=params, **kwargs
    )


def shaped(*dims, dtype=f32):
    return jax.ShapeDtypeStruct(dims, dtype)


def fetch_kernel(first, source, target, turned, sems):
    pieces = sems.shape[0]
    span = target.shape[0] // pieces
    copies = []
    for piece in range(pieces):
        taken = source.at[pl.ds(first + piece * span, span)]
        placed = target.at[pl.ds(piece * span, span)]
        copies.append(pltpu.make_async_copy(taken, placed, sems.at[piece]))
    for copy in copies:
        copy.start()
    for piece, copy in enumerate(copies):
        copy.wait()
        for wave in range(piece * span, (piece + 1) * span):
            turned[wave] = target[wave].T


def strip_kernel(sea, east, north, depth, mask, loading, near, away, wet, sems):
    odd = lax.axis_index("lon") & 1
    rows = sea.shape[0]
    copies = [pltpu.make_async_copy(mask, wet, sems.at[0, 4])]
    for side, target in enumerate((near, away)):
        start = (1 - odd if side == 0 else odd) * (rows - MARGIN)
        span = pl.ds(pl.multiple_of(start, MARGIN), MARGIN)
        for index, source in ((0, sea), (1, east), (2, north), (3, depth), (5, loading)):
            copies.append(
                pltpu.make_async_copy(source.at[span], target.at[index], sems.at[side, index])
            )
    for copy in copies:
        copy.start()
    for copy in copies:
        copy.wait()
    for index in range(rows // MARGIN):
        near[6 + index] = wet[index * MARGIN : (index + 1) * MARGIN].astype(f32)
    first = near[6]
    last = near[5 + rows // MARGIN]
    near[4] = jnp.where(odd > 0, first, last)
    away[4] = jnp.where(odd > 0, last, first)


def pack_kernel(sea, east, north, depth, mask, loading, own, *rest):
    strips = rest[:-3]
    wet, sems, wet_sem = rest[-3:]
    copies = [pltpu.make_async_copy(mask, wet, wet_sem)]
    for index, ref in ((0, sea), (1, east), (2, north), (3, depth), (5, loading)):
        copies.append(pltpu.make_async_copy(ref, own.at[index], sems.at[index]))
    for copy in copies:
        copy.start()
    lat_index = lax.axis_index("lat")
    lat_dev = sea.shape[1]
    for copy in copies:
        copy.wait()
    own[4] = wet[...].astype(f32)
    for index in range(6):
        turned = own[index].T
        top = turned[lat_dev - MARGIN :]
        bottom = turned[:MARGIN]
        if len(strips) == 1:
            strips[0][index] = jnp.where(lat_index == 0, top, bottom)
        else:
            strips[0][index] = top
            strips[1][index] = bottom


def turns_trig(turns, total_cols):
    angle = (2.0 * math.pi / total_cols) * (turns % total_cols).astype(f32)
    return jnp.cos(angle), jnp.sin(angle)


def owners(piece, lon_index, gens):
    owner = jnp.zeros(piece.shape, jnp.int32) + lon_index
    for place, gen in enumerate(gens):
        owner = owner ^ (((piece >> (len(gens) - 1 - place)) & 1) * gen)
    return owner


def join_kernel(own, near, away, *rest):
    count = len(rest) // 2
    sources, targets, wet_pair = rest[:count], rest[count:-1], rest[-1]
    lon_dev, lat_dev = own.shape[1:]
    wet_pair[:lon_dev] = own[4].astype(bf16)
    for index in range(0, lon_dev // MARGIN, 2):
        both = jnp.concatenate([near[6 + index], near[7 + index]], axis=0)
        at = lon_dev + index * MARGIN
        wet_pair[at : at + 2 * MARGIN] = both.astype(bf16)
    lane = lax.broadcasted_iota(jnp.int32, (MARGIN, lat_dev), 1)
    edge = jnp.logical_or(lane < MARGIN, lane >= lat_dev - MARGIN)
    for index in range(6):
        corner = jnp.where(edge, near[index], pltpu.roll(away[index], lat_dev // 2, axis=1))
        for source, target in zip(sources, targets):
            target[index] = source[index]
            target[6 + index] = corner


def table_kernel(
    sizes,
    amp_in,
    phase_in,
    love_in,
    counts_in,
    forward,
    inverse,
    forcing,
    latitude_out,
    love_out,
    counts_out,
    amp,
    phase,
    outer,
    sems,
):
    lon_dev, lat_dev, total_cols, total_rows, wave_dev, gens = sizes
    pairs = ((amp_in, amp), (phase_in, phase), (love_in, love_out), (counts_in, counts_out))
    copies = [
        pltpu.make_async_copy(source, target, sems.at[place])
        for place, (source, target) in enumerate(pairs)
    ]
    for copy in copies:
        copy.start()
    lon_index = lax.axis_index("lon")
    lat_index = lax.axis_index("lat")
    chunk = 2 * wave_dev
    chunks = 1 << len(gens)
    scale = 1.0 / math.sqrt(total_cols)

    def trig(turns):
        return turns_trig(turns, total_cols)

    columns = lon_index * lon_dev + lax.broadcasted_iota(jnp.int32, (wave_dev, lon_dev), 1)
    wave = lax.broadcasted_iota(jnp.int32, (wave_dev, lon_dev), 0)
    cos_in, sin_in = trig(wave * columns)
    cos_in = cos_in * scale
    sin_in = sin_in * scale
    columns = lon_index * lon_dev + lax.broadcasted_iota(jnp.int32, (chunks, lon_dev), 1)
    piece = lax.broadcasted_iota(jnp.int32, (chunks, lon_dev), 0)
    owner = owners(piece, lon_index, gens)
    cos_out, sin_out = trig(owner * wave_dev * columns)
    outer[0] = cos_out
    outer[1] = sin_out
    block = LANES // chunk

    def fill(index, _):
        rows = []
        for inner in range(block):
            at = pl.ds(index * block + inner, 1)
            cos_at, sin_at = outer[0, at], outer[1, at]
            rows.append(cos_at * cos_in - sin_at * sin_in)
            rows.append(-(sin_at * cos_in + cos_at * sin_in))
        rows = jnp.concatenate(rows, axis=0)
        high, low = split_bf16(rows)
        span = pl.ds(pl.multiple_of(index * LANES, LANES), LANES)
        forward[span, :lon_dev] = high
        forward[span, lon_dev:] = low
        high_t, low_t = split_bf16(rows.T)
        inverse[:lon_dev, span] = high_t
        inverse[lon_dev:, span] = low_t
        return 0

    lax.fori_loop(0, chunks // block, fill, 0)
    wide = lon_dev + 2 * MARGIN
    lane = lax.broadcasted_iota(jnp.int32, (8, 2 * lat_dev), 1)
    row = jnp.where(lane < lat_dev + lat_dev // 2, lane, lane - 2 * lat_dev) + lat_index * lat_dev
    latitude = -lat_edge + 2.0 * lat_edge * (row.astype(f32) + 0.5) / total_rows
    inside = jnp.clip(latitude, -1.5, 1.5)
    cosine = jnp.cos(inside)
    latitude_out[0] = cosine
    latitude_out[1] = 1.0 / cosine
    latitude_out[2] = rotation * jnp.sin(inside)
    semi = jnp.cos(latitude) ** 2
    diurnal = jnp.sin(2.0 * latitude)

    spot = lax.broadcasted_iota(jnp.int32, (8, wide), 1)
    order = 1 + (lax.broadcasted_iota(jnp.int32, (8, wide), 0) & 1)
    spot = jnp.where(spot < lon_dev + MARGIN, spot, spot - wide) + lon_index * lon_dev
    cos_lon, sin_lon = trig(spot * order + total_cols * 2)
    both = jnp.concatenate([cos_lon, sin_lon], axis=0).T
    cos_one, cos_two = both[:, 0:1], both[:, 1:2]
    sin_one, sin_two = both[:, 8:9], both[:, 9:10]

    count = len(frequencies)
    place = lax.broadcasted_iota(jnp.int32, (8, count), 1)
    moment = lax.broadcasted_iota(jnp.int32, (8, count), 0).astype(f32)
    omega = jnp.zeros((8, count), f32)
    for index in range(count):
        omega = jnp.where(place == index, frequencies[index], omega)
    for copy in copies:
        copy.wait()
    argument = omega * moment + phase[...]
    strength = amp[...] * (total_cols / 64.0)
    real = strength * jnp.cos(argument)
    imag = strength * jnp.sin(argument)
    is_semi = place < diurnal_from

    def total(values, chosen):
        return jnp.sum(jnp.where(chosen, values, 0.0), axis=1, keepdims=True)

    semi_real = total(real, is_semi)
    semi_imag = total(imag, is_semi)
    diurnal_real = total(real, jnp.logical_not(is_semi))
    diurnal_imag = total(imag, jnp.logical_not(is_semi))
    for k in range(SUBSTEPS):
        at = slice(k, k + 1)
        along = cos_two * semi_real[at] - sin_two * semi_imag[at]
        across = cos_one * diurnal_real[at] - sin_one * diurnal_imag[at]
        forcing[k] = along * semi[0:1] + across * diurnal[0:1]


def mask_kernel(sizes, pair, far, keep, send):
    lon_dev, total_cols, wave_dev, gens = sizes
    lon_index = lax.axis_index("lon")
    chunks = 1 << (len(gens) - 2)
    scale = 1.0 / math.sqrt(total_cols)
    column = lax.broadcasted_iota(jnp.int32, (wave_dev, lon_dev), 1)
    wave = lax.broadcasted_iota(jnp.int32, (wave_dev, lon_dev), 0)
    spot = lax.broadcasted_iota(jnp.int32, (chunks, lon_dev), 1)
    piece = lax.broadcasted_iota(jnp.int32, (chunks, lon_dev), 0)
    owner = owners(piece, lon_index, gens[2:])
    result = None
    for source, other in ((pair, 0), (far, gens[1])):
        for at, offset in ((0, other), (1, other ^ gens[0])):
            start = (lon_index ^ offset) * lon_dev
            cos_in, sin_in = turns_trig(wave * (column + start), total_cols)
            cos_in = cos_in * scale
            sin_in = sin_in * scale
            cos_out, sin_out = turns_trig(owner * wave_dev * (spot + start), total_cols)
            rows = []
            for index in range(chunks):
                cos_at, sin_at = cos_out[index : index + 1], sin_out[index : index + 1]
                rows.append(cos_at * cos_in - sin_at * sin_in)
                rows.append(-(sin_at * cos_in + cos_at * sin_in))
            high, low = split_bf16(jnp.concatenate(rows, axis=0))
            wet = source[at * lon_dev : (at + 1) * lon_dev]
            term = jnp.dot(
                jnp.concatenate([high, low], axis=1),
                jnp.concatenate([wet, wet], axis=0),
                preferred_element_type=f32,
            )
            result = term if result is None else result + term
    half = keep.shape[0]
    keep[...] = result[:half]
    send[...] = result[half:]


def along(f):
    return pltpu.roll(f, f.shape[0] - 1, axis=0) - pltpu.roll(f, 1, axis=0)


def across(f):
    return pltpu.roll(f, f.shape[1] - 1, axis=1) - pltpu.roll(f, 1, axis=1)


def rise(state, static, rows):
    cosine, secant, _ = rows
    depth = static[0]
    divergence = (along(depth * state[1]) + across(depth * state[2] * cosine)) * 0.5 * secant
    state[0] = state[0] - courant * divergence * static[1]


def veer(state, static, forcing, rows):
    _, secant, coriolis = rows
    east = state[1]
    north = state[2]
    wet = static[1]
    pressure = state[0] - forcing - static[2]
    slope_east = along(pressure) * 0.5 * secant
    slope_north = across(pressure) * 0.5
    return (
        wet * ((1.0 - friction) * east + courant * (coriolis * north - slope_east)),
        wet * ((1.0 - friction) * north - courant * (coriolis * east + slope_north)),
    )


def step_kernel(count, own, near, away, *rest):
    facing = rest[: 1 if count == 2 else 2]
    (
        forcing,
        latitude,
        forward,
        keep,
        send,
        wet_sum,
        state,
        static,
    ) = rest[len(facing) :]
    above, below = facing[0], facing[-1]
    lon_dev, lat_dev = own.shape[1:]
    lat_index = lax.axis_index("lat")
    odd = (lax.axis_index("lon") & 1) > 0
    has_top = lat_index < count - 1
    has_bottom = lat_index > 0
    middle = jnp.zeros((lat_dev - 2 * MARGIN, lon_dev), f32)
    lane = lax.broadcasted_iota(jnp.int32, (MARGIN, lat_dev), 1)
    at_top = jnp.logical_and(lane < MARGIN, has_top)
    at_bottom = jnp.logical_and(lane >= lat_dev - MARGIN, has_bottom)

    fields = []
    for index in range(6):
        cells = own[index]
        north_rows = jnp.where(has_top, above[index], 0.0)
        south_rows = jnp.where(has_bottom, below[index], 0.0)
        side = jnp.concatenate([north_rows, middle, south_rows], axis=0).T
        corners = []
        for turn in (0, lat_dev // 2):
            north_part, south_part = above[6 + index], below[6 + index]
            if turn:
                north_part = pltpu.roll(north_part, turn, axis=1)
                south_part = pltpu.roll(south_part, turn, axis=1)
            part = jnp.where(at_bottom, south_part, 0.0)
            corners.append(jnp.where(at_top, north_part, part))
        corner_east = jnp.where(odd, corners[1], corners[0])
        corner_west = jnp.where(odd, corners[0], corners[1])
        from_east = jnp.where(odd, away[index], near[index])
        from_west = jnp.where(odd, near[index], away[index])
        left = jnp.concatenate([cells, from_east, from_west], axis=0)
        right = jnp.concatenate([side, corner_east, corner_west], axis=0)
        fields.append(jnp.concatenate([left, right], axis=1))
    for index in range(3):
        state[index] = fields[index]
        static[index] = fields[3 + index]

    rows = tuple(latitude[index][0:1] for index in range(3))

    def substep(k):
        rise(state, static, rows)
        state[1], state[2] = veer(state, static, forcing[k], rows)
        return 0

    for k in range(SUBSTEPS - 1):
        substep(k)
    rise(state, static, rows)
    product = state[0, :lon_dev, :lat_dev] * own[4]
    level = jnp.sum(jnp.sum(product, axis=0, keepdims=True), axis=1, keepdims=True)
    level = jnp.broadcast_to(level, wet_sum.shape)
    wet_sum[...] = level
    high, low = split_bf16(product)
    upper = jnp.concatenate([high, low], axis=1)
    under = jnp.concatenate([high, jnp.zeros_like(low)], axis=1)
    weights = jnp.concatenate([upper, under], axis=0)
    half = keep.shape[0]

    def transform(span):
        both = jnp.dot(forward[span], weights, preferred_element_type=f32)
        return both[:, :lat_dev] + both[:, lat_dev:]

    send[:half] = transform(slice(half, 2 * half))
    send[half:] = level
    keep[...] = transform(slice(0, half))


def finish_kernel(state, static, forcing, latitude, height_out, east_out, north_out):
    lon_dev, lat_dev = height_out.shape
    rows = tuple(latitude[index][0:1] for index in range(3))
    east, north = veer(state, static, forcing[SUBSTEPS - 1], rows)
    height_out[...] = state[0, :lon_dev, :lat_dev]
    east_out[...] = east[:lon_dev, :lat_dev]
    north_out[...] = north[:lon_dev, :lat_dev]


GROUP = 8


def pair(legendre, wave):
    return jnp.concatenate([legendre[wave], legendre[wave + 1]], axis=1)


def locate(table, second, wave):
    held = table.shape[0]
    return (table, wave) if wave < held else (second, wave - held)


def analysis_kernel(sizes, keep, recv, wet_keep, wet_sum, wet_counts, table, second, *outs):
    first, waves = sizes
    lat_dev = keep.shape[1]
    rows = keep.shape[0]
    counts = wet_counts[...].astype(f32)
    total = jnp.sum(jnp.sum(counts, axis=1, keepdims=True), axis=0, keepdims=True)
    mean = wet_sum[0:1, 0:1] / total
    lines = 2 * GROUP
    line = lax.broadcasted_iota(jnp.int32, (lines, lat_dev), 0) & (GROUP - 1)
    for group in range(waves // GROUP):
        values = []
        for begin in (first + group * GROUP, rows // 2 + first + group * GROUP):
            span = slice(begin, begin + GROUP)
            wet_span = slice(rows + begin, rows + begin + GROUP)
            values.append((keep[span] + recv[span]) - mean * (wet_keep[span] + recv[wet_span]))
        value = jnp.concatenate(values, axis=0)
        result = None
        for step in range(0, GROUP, 2):
            left = jnp.concatenate(
                [
                    jnp.where(line == step, value, 0.0).astype(bf16),
                    jnp.where(line == step + 1, value, 0.0).astype(bf16),
                ],
                axis=1,
            )
            source, wave = locate(table, second, first + group * GROUP + step)
            right = jnp.concatenate([source[wave], source[wave + 1]], axis=0)
            term = jnp.dot(left, right, preferred_element_type=f32)
            result = term if result is None else result + term
        for target in outs:
            target[group * lines : (group + 1) * lines] = result.astype(target.dtype)


def synthesis_kernel(sizes, own, recv, love, table, second, *rest):
    first, waves, wave_dev = sizes
    out = rest[-1]
    lead = rest[:-1]
    lat_dev = out.shape[1]
    lines = 2 * GROUP
    line = lax.broadcasted_iota(jnp.int32, (lines, lat_dev), 0) & (GROUP - 1)
    base = lax.axis_index("lon") * wave_dev + first
    real, imag = [], []
    for group in range(waves // GROUP):
        span = slice(group * lines, (group + 1) * lines)
        total = own[span].astype(f32) + recv[span].astype(f32)
        scaled = (love[...] * total).astype(bf16)
        result = None
        for step in range(0, GROUP, 2):
            source, wave = locate(table, second, first + group * GROUP + step)
            both = jnp.dot(scaled, pair(source, wave), preferred_element_type=f32)
            left, right = both[:, :lat_dev], both[:, lat_dev:]
            result = left if result is None else jnp.where(line == step, left, result)
            result = jnp.where(line == step + 1, right, result)
        result = jnp.where(base + group * GROUP + line == 0, 1.0, 2.0) * result
        real.append(result[:GROUP])
        imag.append(result[GROUP:])
    if lead:
        half = lead[0].shape[0] // 2
        real.insert(0, lead[0][:half])
        imag.insert(0, lead[0][half:])
    out[...] = jnp.concatenate(real + imag, axis=0).astype(out.dtype)


def inverse_near_kernel(inverse, near, out):
    half = near.shape[0]
    out[...] = jnp.dot(inverse[:, :half], near[...], preferred_element_type=f32)


def inverse_far_kernel(inverse, started, far, out):
    lon_dev = out.shape[0]
    half = far.shape[0]
    both = started[...] + jnp.dot(inverse[:, half:], far[...], preferred_element_type=f32)
    out[...] = both[:lon_dev] + both[lon_dev:]


def shards(
    sea_level,
    east_velocity,
    north_velocity,
    depth,
    land_mask,
    wet_counts,
    loading_prev,
    tide_amp,
    tide_phase,
    legendre,
    love_factor,
):
    lon_dev, lat_dev = sea_level.shape
    wave_dev, degrees = legendre.shape[:2]
    lon_count = lax.axis_size("lon")
    lat_count = lax.axis_size("lat")
    total_cols = lon_dev * lon_count
    total_rows = lat_dev * lat_count
    bits = lon_count.bit_length() - 1
    lat_bits = lat_count.bit_length() - 1
    assert lon_count == 1 << bits and lat_count == 1 << lat_bits
    gens = [1] + [(1 << b) ^ 1 for b in (1, *range(bits - 1, 1, -1))][: bits - 1]
    vmem = pl.BlockSpec(memory_space=pltpu.VMEM)
    hbm = pl.BlockSpec(memory_space=pltpu.HBM)

    strip = shaped(6, MARGIN, LANES)

    def stay_put(cells):
        return pltpu.with_memory_space_constraint(cells, pltpu.HBM)

    fields = tuple(
        map(stay_put, (sea_level, east_velocity, north_velocity, depth, land_mask, loading_prev))
    )
    near, away = call(
        strip_kernel,
        [shaped(6 + lon_dev // MARGIN, MARGIN, LANES), strip],
        in_specs=[hbm] * 6,
        scratch=[
            pltpu.VMEM((lon_dev, lat_dev), jnp.int32),
            pltpu.SemaphoreType.DMA((2, 6)),
        ],
    )(*fields)
    own, *strips = call(
        pack_kernel,
        [shaped(6, lon_dev, lat_dev)] + [strip] * (1 if lat_count == 2 else 2),
        in_specs=[hbm] * 6,
        scratch=[
            pltpu.VMEM((lon_dev, lat_dev), jnp.int32),
            pltpu.SemaphoreType.DMA((6,)),
            pltpu.SemaphoreType.DMA,
        ],
    )(*fields)

    def stay(b):
        return b

    def nearby(b):
        return b ^ 1

    def beyond(b):
        return (b + 1 if b & 1 else b - 1) % lon_count

    def shift(cells, lat_step, move):
        pairs = []
        for a in range(lat_count):
            target = a ^ 1 if lat_step is None else a + lat_step
            if 0 <= target < lat_count:
                for b in range(lon_count):
                    pairs.append((a * lon_count + b, target * lon_count + move(b)))
        return lax.ppermute(cells, ("lat", "lon"), pairs)

    away = shift(away, 0, beyond)
    near = shift(near, 0, nearby)

    *strips, wet_pair = call(
        join_kernel,
        [shaped(12, MARGIN, LANES)] * len(strips)
        + [shaped(2 * lon_dev, lat_dev, dtype=bf16)],
    )(own, near, away, *strips)
    if lat_count == 2:
        facing = [shift(strips[0], None, stay)]
    else:
        facing = [shift(strips[1], -1, stay), shift(strips[0], 1, stay)]
    chunk = 2 * wave_dev
    lines = chunk * lon_count
    half = lines // 2
    wide = lon_dev + 2 * MARGIN
    forward, inverse, forcing, latitude, love, counts = call(
        functools.partial(
            table_kernel, (lon_dev, lat_dev, total_cols, total_rows, wave_dev, tuple(gens))
        ),
        [
            shaped(lines, 2 * lon_dev, dtype=bf16),
            shaped(2 * lon_dev, lines, dtype=bf16),
            shaped(SUBSTEPS, wide, 2 * lat_dev),
            shaped(3, 8, 2 * lat_dev),
            shaped(1, degrees),
            shaped(*wet_counts.shape, dtype=jnp.int32),
        ],
        in_specs=[hbm] * 4,
        scratch=[
            pltpu.VMEM((1, len(frequencies)), f32),
            pltpu.VMEM((1, len(frequencies)), f32),
            pltpu.VMEM((2, lon_count, lon_dev), f32),
            pltpu.SemaphoreType.DMA((4,)),
        ],
    )(
        stay_put(tide_amp[None]),
        stay_put(tide_phase[None]),
        stay_put(love_factor[None]),
        stay_put(wet_counts),
    )

    def swap(cells, gen):
        return lax.ppermute(cells, "lon", [(i, i ^ gen) for i in range(lon_count)])

    wet_far = swap(wet_pair, gens[1])

    keep, send, wet_sum, state, static = call(
        functools.partial(step_kernel, lat_count),
        [shaped(half, lat_dev), shaped(half + 8, lat_dev), shaped(8, lat_dev)]
        + [pltpu.VMEM((3, wide, 2 * lat_dev), f32)] * 2,
        in_specs=[vmem] * (6 + len(facing)),
    )(own, near, away, *facing, forcing, latitude, forward)

    recv = swap(send, gens[0])
    wet_keep, wet_send = call(
        functools.partial(mask_kernel, (lon_dev, total_cols, wave_dev, tuple(gens))),
        [shaped(half // 4, lat_dev)] * 2,
    )(wet_pair, wet_far)
    wet_recv = swap(wet_send, gens[2])
    level = wet_sum + recv[half:]
    joined = lat_count == 2
    part = half // 2
    send = jnp.concatenate([keep[part:] + recv[part:half], level], axis=0)
    keep = keep[:part] + recv[:part]
    recv = swap(send, gens[1])
    arrived = recv[part:]
    if joined:
        arrived = arrived + shift(level, None, nearby)
        arrived = arrived + shift(level, None, lambda b: b ^ gens[1])
    level = level + arrived
    for place, gen in enumerate(gens[2:]):
        part = keep.shape[0] // 2
        sends = [keep[part:] + recv[part : 2 * part]]
        keep = keep[:part] + recv[:part]
        if place > 0:
            sends.append(wet_keep[part:] + wet_recv[part : 2 * part])
            wet_keep = wet_keep[:part] + wet_recv[:part]
        recv = swap(jnp.concatenate([*sends, level], axis=0), gen)
        if place > 0:
            wet_recv = recv[part : 2 * part]
            level = level + recv[2 * part :]
        else:
            level = level + recv[part:]
    if not joined:
        for b in range(lat_bits):
            level = level + lax.ppermute(
                level, "lat", [(i, i ^ (1 << b)) for i in range(lat_count)]
            )

    parts = 2
    waves = wave_dev // parts
    tables = []
    for piece in range(parts):
        tables.append(
            call(
                functools.partial(fetch_kernel, piece * waves),
                [
                    pltpu.VMEM((waves, degrees, lat_dev), bf16),
                    pltpu.VMEM((waves, lat_dev, degrees), bf16),
                ],
                in_specs=[hbm],
                scratch=[pltpu.SemaphoreType.DMA((4,))],
            )(stay_put(legendre))
        )
    turned = [table[1] for table in tables]
    tables = [table[0] for table in tables]
    pieces = ((0, wave_dev - wave_dev // 4), (wave_dev - wave_dev // 4, wave_dev // 4))
    sums = []
    for first, waves in pieces:
        mine, moving = call(
            functools.partial(analysis_kernel, (first, waves)),
            [shaped(2 * waves, degrees), shaped(2 * waves, degrees, dtype=bf16)],
            in_specs=[vmem] * 7,
        )(keep, recv, wet_keep, level, counts, *turned)
        for b in range(lat_bits):
            other = lax.ppermute(moving, "lat", [(i, i ^ (1 << b)) for i in range(lat_count)])
            if b < lat_bits - 1:
                mine = mine + other.astype(f32)
                moving = mine.astype(bf16)
        sums.append((mine, other))
    spectra = ()
    for piece, (first, waves) in enumerate(pieces):
        last = piece == len(pieces) - 1
        spectra = (
            call(
                functools.partial(synthesis_kernel, (first, waves, wave_dev)),
                shaped(2 * (first + waves), lat_dev, dtype=bf16 if last else f32),
                in_specs=[vmem] * (5 + len(spectra)),
            )(*sums[piece], love, *tables, *spectra),
        )
    near = spectra[0]
    for gen in gens[:0:-1]:
        near = jnp.concatenate([near, swap(near, gen)], axis=0)
    far = swap(near, gens[0])
    started = call(inverse_near_kernel, shaped(2 * lon_dev, lat_dev))(inverse, near)
    loading_new = call(inverse_far_kernel, shaped(lon_dev, lat_dev))(inverse, started, far)
    height, east_new, north_new = call(finish_kernel, [shaped(lon_dev, lat_dev)] * 3)(
        state, static, forcing, latitude
    )
    return (height, east_new, north_new, loading_new)


def solution(mesh):
    tile = P("lon", "lat")
    return jax.shard_map(
        shards,
        mesh=mesh,
        in_specs=(tile,) * 5 + (P(), tile, P(), P(), P("lon", None, "lat"), P()),
        out_specs=(tile,) * 4,
        check_vma=False,
    )
```

```python
import functools
import math

import jax
import jax.numpy as jnp
from jax import lax
from jax.experimental import pallas as pl
from jax.experimental.pallas import tpu as pltpu
from jax.sharding import PartitionSpec as P


SUBSTEPS = 4
MARGIN = 2 * SUBSTEPS

lat_edge = 1.3089969
courant = 0.4
friction = 0.02
rotation = 0.2
frequencies = (0.1405, 0.1454, 0.1379, 0.1458, 0.0729, 0.0676, 0.0725, 0.0649)
diurnal_from = 4

f32 = jnp.float32
bf16 = jnp.bfloat16
LANES = 128


def split_bf16(x):
    high = x.astype(bf16)
    return high, (x - high.astype(f32)).astype(bf16)


def call(kernel, out_shape, in_specs=None, scratch=(), vmem=None):
    params = pltpu.CompilerParams(vmem_limit_bytes=(vmem or 16) << 20)
    kwargs = {} if in_specs is None else {"in_specs": in_specs}
    return pl.pallas_call(
        kernel, out_shape=out_shape, scratch_shapes=scratch, compiler_params=params, **kwargs
    )


def shaped(*dims, dtype=f32):
    return jax.ShapeDtypeStruct(dims, dtype)


def fetch_kernel(first, source, target, turned, sems):
    pieces = sems.shape[0]
    span = target.shape[0] // pieces
    copies = []
    for piece in range(pieces):
        taken = source.at[pl.ds(first + piece * span, span)]
        placed = target.at[pl.ds(piece * span, span)]
        copies.append(pltpu.make_async_copy(taken, placed, sems.at[piece]))
    for copy in copies:
        copy.start()
    for piece, copy in enumerate(copies):
        copy.wait()
        for wave in range(piece * span, (piece + 1) * span):
            turned[wave] = target[wave].T


def strip_kernel(sea, east, north, depth, mask, loading, near, away, wet, sems):
    odd = lax.axis_index("lon") & 1
    rows = sea.shape[0]
    copies = [pltpu.make_async_copy(mask, wet, sems.at[0, 4])]
    for side, target in enumerate((near, away)):
        start = (1 - odd if side == 0 else odd) * (rows - MARGIN)
        span = pl.ds(pl.multiple_of(start, MARGIN), MARGIN)
        for index, source in ((0, sea), (1, east), (2, north), (3, depth), (5, loading)):
            copies.append(
                pltpu.make_async_copy(source.at[span], target.at[index], sems.at[side, index])
            )
    for copy in copies:
        copy.start()
    for copy in copies:
        copy.wait()
    for index in range(rows // MARGIN):
        near[6 + index] = wet[index * MARGIN : (index + 1) * MARGIN].astype(f32)
    first = near[6]
    last = near[5 + rows // MARGIN]
    near[4] = jnp.where(odd > 0, first, last)
    away[4] = jnp.where(odd > 0, last, first)


def pack_kernel(sea, east, north, depth, mask, loading, own, *rest):
    strips = rest[:-3]
    wet, sems, wet_sem = rest[-3:]
    copies = [pltpu.make_async_copy(mask, wet, wet_sem)]
    for index, ref in ((0, sea), (1, east), (2, north), (3, depth), (5, loading)):
        copies.append(pltpu.make_async_copy(ref, own.at[index], sems.at[index]))
    for copy in copies:
        copy.start()
    lat_index = lax.axis_index("lat")
    lat_dev = sea.shape[1]
    for copy in copies:
        copy.wait()
    own[4] = wet[...].astype(f32)
    for index in range(6):
        turned = own[index].T
        top = turned[lat_dev - MARGIN :]
        bottom = turned[:MARGIN]
        if len(strips) == 1:
            strips[0][index] = jnp.where(lat_index == 0, top, bottom)
        else:
            strips[0][index] = top
            strips[1][index] = bottom


def turns_trig(turns, total_cols):
    angle = (2.0 * math.pi / total_cols) * (turns % total_cols).astype(f32)
    return jnp.cos(angle), jnp.sin(angle)


def owners(piece, lon_index, gens):
    owner = jnp.zeros(piece.shape, jnp.int32) + lon_index
    for place, gen in enumerate(gens):
        owner = owner ^ (((piece >> (len(gens) - 1 - place)) & 1) * gen)
    return owner


def join_kernel(own, near, away, *rest):
    count = len(rest) // 2
    sources, targets, wet_pair = rest[:count], rest[count:-1], rest[-1]
    lon_dev, lat_dev = own.shape[1:]
    wet_pair[:lon_dev] = own[4].astype(bf16)
    for index in range(0, lon_dev // MARGIN, 2):
        both = jnp.concatenate([near[6 + index], near[7 + index]], axis=0)
        at = lon_dev + index * MARGIN
        wet_pair[at : at + 2 * MARGIN] = both.astype(bf16)
    lane = lax.broadcasted_iota(jnp.int32, (MARGIN, lat_dev), 1)
    edge = jnp.logical_or(lane < MARGIN, lane >= lat_dev - MARGIN)
    for index in range(6):
        corner = jnp.where(edge, near[index], pltpu.roll(away[index], lat_dev // 2, axis=1))
        for source, target in zip(sources, targets):
            target[index] = source[index]
            target[6 + index] = corner


def table_kernel(
    sizes,
    amp_in,
    phase_in,
    love_in,
    counts_in,
    forward,
    inverse,
    forcing,
    latitude_out,
    love_out,
    counts_out,
    amp,
    phase,
    outer,
    sems,
):
    lon_dev, lat_dev, total_cols, total_rows, wave_dev, gens = sizes
    pairs = ((amp_in, amp), (phase_in, phase), (love_in, love_out), (counts_in, counts_out))
    copies = [
        pltpu.make_async_copy(source, target, sems.at[place])
        for place, (source, target) in enumerate(pairs)
    ]
    for copy in copies:
        copy.start()
    lon_index = lax.axis_index("lon")
    lat_index = lax.axis_index("lat")
    chunk = 2 * wave_dev
    chunks = 1 << len(gens)
    scale = 1.0 / math.sqrt(total_cols)

    def trig(turns):
        return turns_trig(turns, total_cols)

    columns = lon_index * lon_dev + lax.broadcasted_iota(jnp.int32, (wave_dev, lon_dev), 1)
    wave = lax.broadcasted_iota(jnp.int32, (wave_dev, lon_dev), 0)
    cos_in, sin_in = trig(wave * columns)
    cos_in = cos_in * scale
    sin_in = sin_in * scale
    columns = lon_index * lon_dev + lax.broadcasted_iota(jnp.int32, (chunks, lon_dev), 1)
    piece = lax.broadcasted_iota(jnp.int32, (chunks, lon_dev), 0)
    owner = owners(piece, lon_index, gens)
    cos_out, sin_out = trig(owner * wave_dev * columns)
    outer[0] = cos_out
    outer[1] = sin_out
    block = LANES // chunk

    def fill(index, _):
        rows = []
        for inner in range(block):
            at = pl.ds(index * block + inner, 1)
            cos_at, sin_at = outer[0, at], outer[1, at]
            rows.append(cos_at * cos_in - sin_at * sin_in)
            rows.append(-(sin_at * cos_in + cos_at * sin_in))
        rows = jnp.concatenate(rows, axis=0)
        high, low = split_bf16(rows)
        span = pl.ds(pl.multiple_of(index * LANES, LANES), LANES)
        forward[span, :lon_dev] = high
        forward[span, lon_dev:] = low
        high_t, low_t = split_bf16(rows.T)
        inverse[:lon_dev, span] = high_t
        inverse[lon_dev:, span] = low_t
        return 0

    lax.fori_loop(0, chunks // block, fill, 0)
    wide = lon_dev + 2 * MARGIN
    lane = lax.broadcasted_iota(jnp.int32, (8, 2 * lat_dev), 1)
    row = jnp.where(lane < lat_dev + lat_dev // 2, lane, lane - 2 * lat_dev) + lat_index * lat_dev
    latitude = -lat_edge + 2.0 * lat_edge * (row.astype(f32) + 0.5) / total_rows
    inside = jnp.clip(latitude, -1.5, 1.5)
    cosine = jnp.cos(inside)
    latitude_out[0] = cosine
    latitude_out[1] = 1.0 / cosine
    latitude_out[2] = rotation * jnp.sin(inside)
    semi = jnp.cos(latitude) ** 2
    diurnal = jnp.sin(2.0 * latitude)

    spot = lax.broadcasted_iota(jnp.int32, (8, wide), 1)
    order = 1 + (lax.broadcasted_iota(jnp.int32, (8, wide), 0) & 1)
    spot = jnp.where(spot < lon_dev + MARGIN, spot, spot - wide) + lon_index * lon_dev
    cos_lon, sin_lon = trig(spot * order + total_cols * 2)
    both = jnp.concatenate([cos_lon, sin_lon], axis=0).T
    cos_one, cos_two = both[:, 0:1], both[:, 1:2]
    sin_one, sin_two = both[:, 8:9], both[:, 9:10]

    count = len(frequencies)
    place = lax.broadcasted_iota(jnp.int32, (8, count), 1)
    moment = lax.broadcasted_iota(jnp.int32, (8, count), 0).astype(f32)
    omega = jnp.zeros((8, count), f32)
    for index in range(count):
        omega = jnp.where(place == index, frequencies[index], omega)
    for copy in copies:
        copy.wait()
    argument = omega * moment + phase[...]
    strength = amp[...] * (total_cols / 64.0)
    real = strength * jnp.cos(argument)
    imag = strength * jnp.sin(argument)
    is_semi = place < diurnal_from

    def total(values, chosen):
        return jnp.sum(jnp.where(chosen, values, 0.0), axis=1, keepdims=True)

    semi_real = total(real, is_semi)
    semi_imag = total(imag, is_semi)
    diurnal_real = total(real, jnp.logical_not(is_semi))
    diurnal_imag = total(imag, jnp.logical_not(is_semi))
    for k in range(SUBSTEPS):
        at = slice(k, k + 1)
        along = cos_two * semi_real[at] - sin_two * semi_imag[at]
        across = cos_one * diurnal_real[at] - sin_one * diurnal_imag[at]
        forcing[k] = along * semi[0:1] + across * diurnal[0:1]


def mask_kernel(sizes, pair, far, keep, send):
    lon_dev, total_cols, wave_dev, gens = sizes
    lon_index = lax.axis_index("lon")
    chunks = 1 << (len(gens) - 2)
    scale = 1.0 / math.sqrt(total_cols)
    column = lax.broadcasted_iota(jnp.int32, (wave_dev, lon_dev), 1)
    wave = lax.broadcasted_iota(jnp.int32, (wave_dev, lon_dev), 0)
    spot = lax.broadcasted_iota(jnp.int32, (chunks, lon_dev), 1)
    piece = lax.broadcasted_iota(jnp.int32, (chunks, lon_dev), 0)
    owner = owners(piece, lon_index, gens[2:])
    result = None
    for source, other in ((pair, 0), (far, gens[1])):
        for at, offset in ((0, other), (1, other ^ gens[0])):
            start = (lon_index ^ offset) * lon_dev
            cos_in, sin_in = turns_trig(wave * (column + start), total_cols)
            cos_in = cos_in * scale
            sin_in = sin_in * scale
            cos_out, sin_out = turns_trig(owner * wave_dev * (spot + start), total_cols)
            rows = []
            for index in range(chunks):
                cos_at, sin_at = cos_out[index : index + 1], sin_out[index : index + 1]
                rows.append(cos_at * cos_in - sin_at * sin_in)
                rows.append(-(sin_at * cos_in + cos_at * sin_in))
            high, low = split_bf16(jnp.concatenate(rows, axis=0))
            wet = source[at * lon_dev : (at + 1) * lon_dev]
            term = jnp.dot(
                jnp.concatenate([high, low], axis=1),
                jnp.concatenate([wet, wet], axis=0),
                preferred_element_type=f32,
            )
            result = term if result is None else result + term
    half = keep.shape[0]
    keep[...] = result[:half]
    send[...] = result[half:]


def along(f):
    return pltpu.roll(f, f.shape[0] - 1, axis=0) - pltpu.roll(f, 1, axis=0)


def across(f):
    return pltpu.roll(f, f.shape[1] - 1, axis=1) - pltpu.roll(f, 1, axis=1)


def rise(state, static, rows):
    cosine, secant, _ = rows
    depth = static[0]
    divergence = (along(depth * state[1]) + across(depth * state[2] * cosine)) * 0.5 * secant
    state[0] = state[0] - courant * divergence * static[1]


def veer(state, static, forcing, rows):
    _, secant, coriolis = rows
    east = state[1]
    north = state[2]
    wet = static[1]
    pressure = state[0] - forcing - static[2]
    slope_east = along(pressure) * 0.5 * secant
    slope_north = across(pressure) * 0.5
    return (
        wet * ((1.0 - friction) * east + courant * (coriolis * north - slope_east)),
        wet * ((1.0 - friction) * north - courant * (coriolis * east + slope_north)),
    )


def step_kernel(count, own, near, away, *rest):
    facing = rest[: 1 if count == 2 else 2]
    (
        forcing,
        latitude,
        forward,
        held,
        send,
        wet_sum,
        state,
        static,
    ) = rest[len(facing) :]
    above, below = facing[0], facing[-1]
    lon_dev, lat_dev = own.shape[1:]
    lat_index = lax.axis_index("lat")
    odd = (lax.axis_index("lon") & 1) > 0
    has_top = lat_index < count - 1
    has_bottom = lat_index > 0
    middle = jnp.zeros((lat_dev - 2 * MARGIN, lon_dev), f32)
    lane = lax.broadcasted_iota(jnp.int32, (MARGIN, lat_dev), 1)
    at_top = jnp.logical_and(lane < MARGIN, has_top)
    at_bottom = jnp.logical_and(lane >= lat_dev - MARGIN, has_bottom)

    fields = []
    for index in range(6):
        cells = own[index]
        north_rows = jnp.where(has_top, above[index], 0.0)
        south_rows = jnp.where(has_bottom, below[index], 0.0)
        side = jnp.concatenate([north_rows, middle, south_rows], axis=0).T
        corners = []
        for turn in (0, lat_dev // 2):
            north_part, south_part = above[6 + index], below[6 + index]
            if turn:
                north_part = pltpu.roll(north_part, turn, axis=1)
                south_part = pltpu.roll(south_part, turn, axis=1)
            part = jnp.where(at_bottom, south_part, 0.0)
            corners.append(jnp.where(at_top, north_part, part))
        corner_east = jnp.where(odd, corners[1], corners[0])
        corner_west = jnp.where(odd, corners[0], corners[1])
        from_east = jnp.where(odd, away[index], near[index])
        from_west = jnp.where(odd, near[index], away[index])
        left = jnp.concatenate([cells, from_east, from_west], axis=0)
        right = jnp.concatenate([side, corner_east, corner_west], axis=0)
        fields.append(jnp.concatenate([left, right], axis=1))
    for index in range(3):
        state[index] = fields[index]
        static[index] = fields[3 + index]

    rows = tuple(latitude[index][0:1] for index in range(3))

    def substep(k):
        rise(state, static, rows)
        state[1], state[2] = veer(state, static, forcing[k], rows)
        return 0

    for k in range(SUBSTEPS - 1):
        substep(k)
    rise(state, static, rows)
    product = state[0, :lon_dev, :lat_dev] * own[4]
    level = jnp.sum(jnp.sum(product, axis=0, keepdims=True), axis=1, keepdims=True)
    level = jnp.broadcast_to(level, wet_sum.shape)
    wet_sum[...] = level
    high, low = split_bf16(product)
    upper = jnp.concatenate([high, low], axis=1)
    under = jnp.concatenate([high, jnp.zeros_like(low)], axis=1)
    weights = jnp.concatenate([upper, under], axis=0)
    half = forward.shape[0] // 2

    def transform(span):
        both = jnp.dot(forward[span], weights, preferred_element_type=f32)
        return both[:, :lat_dev] + both[:, lat_dev:]

    send[:half] = transform(slice(half, 2 * half))
    send[half:] = level
    held[...] = weights


def keep_kernel(forward, weights, keep):
    half, lat_dev = keep.shape
    both = jnp.dot(forward[:half], weights[...], preferred_element_type=f32)
    keep[...] = both[:, :lat_dev] + both[:, lat_dev:]


def finish_kernel(state, static, forcing, latitude, height_out, east_out, north_out):
    lon_dev, lat_dev = height_out.shape
    rows = tuple(latitude[index][0:1] for index in range(3))
    east, north = veer(state, static, forcing[SUBSTEPS - 1], rows)
    height_out[...] = state[0, :lon_dev, :lat_dev]
    east_out[...] = east[:lon_dev, :lat_dev]
    north_out[...] = north[:lon_dev, :lat_dev]


GROUP = 8


def pair(legendre, wave):
    return jnp.concatenate([legendre[wave], legendre[wave + 1]], axis=1)


def locate(table, second, wave):
    held = table.shape[0]
    return (table, wave) if wave < held else (second, wave - held)


def analysis_kernel(sizes, keep, recv, wet_keep, wet_sum, wet_counts, table, second, *outs):
    first, waves = sizes
    lat_dev = keep.shape[1]
    rows = keep.shape[0]
    counts = wet_counts[...].astype(f32)
    total = jnp.sum(jnp.sum(counts, axis=1, keepdims=True), axis=0, keepdims=True)
    mean = wet_sum[0:1, 0:1] / total
    lines = 2 * GROUP
    line = lax.broadcasted_iota(jnp.int32, (lines, lat_dev), 0) & (GROUP - 1)
    for group in range(waves // GROUP):
        values = []
        for begin in (first + group * GROUP, rows // 2 + first + group * GROUP):
            span = slice(begin, begin + GROUP)
            wet_span = slice(rows + begin, rows + begin + GROUP)
            values.append((keep[span] + recv[span]) - mean * (wet_keep[span] + recv[wet_span]))
        value = jnp.concatenate(values, axis=0)
        result = None
        for step in range(0, GROUP, 2):
            left = jnp.concatenate(
                [
                    jnp.where(line == step, value, 0.0).astype(bf16),
                    jnp.where(line == step + 1, value, 0.0).astype(bf16),
                ],
                axis=1,
            )
            source, wave = locate(table, second, first + group * GROUP + step)
            right = jnp.concatenate([source[wave], source[wave + 1]], axis=0)
            term = jnp.dot(left, right, preferred_element_type=f32)
            result = term if result is None else result + term
        for target in outs:
            target[group * lines : (group + 1) * lines] = result.astype(target.dtype)


def synthesis_kernel(sizes, own, recv, love, table, second, *rest):
    first, waves, wave_dev = sizes
    out = rest[-1]
    lead = rest[:-1]
    lat_dev = out.shape[1]
    lines = 2 * GROUP
    line = lax.broadcasted_iota(jnp.int32, (lines, lat_dev), 0) & (GROUP - 1)
    base = lax.axis_index("lon") * wave_dev + first
    real, imag = [], []
    for group in range(waves // GROUP):
        span = slice(group * lines, (group + 1) * lines)
        total = own[span].astype(f32) + recv[span].astype(f32)
        scaled = (love[...] * total).astype(bf16)
        result = None
        for step in range(0, GROUP, 2):
            source, wave = locate(table, second, first + group * GROUP + step)
            both = jnp.dot(scaled, pair(source, wave), preferred_element_type=f32)
            left, right = both[:, :lat_dev], both[:, lat_dev:]
            result = left if result is None else jnp.where(line == step, left, result)
            result = jnp.where(line == step + 1, right, result)
        result = jnp.where(base + group * GROUP + line == 0, 1.0, 2.0) * result
        real.append(result[:GROUP])
        imag.append(result[GROUP:])
    if lead:
        half = lead[0].shape[0] // 2
        real.insert(0, lead[0][:half])
        imag.insert(0, lead[0][half:])
    out[...] = jnp.concatenate(real + imag, axis=0).astype(out.dtype)


def inverse_near_kernel(inverse, near, out):
    half = near.shape[0]
    out[...] = jnp.dot(inverse[:, :half], near[...], preferred_element_type=f32)


def inverse_far_kernel(inverse, started, far, out):
    lon_dev = out.shape[0]
    half = far.shape[0]
    both = started[...] + jnp.dot(inverse[:, half:], far[...], preferred_element_type=f32)
    out[...] = both[:lon_dev] + both[lon_dev:]


def shards(
    sea_level,
    east_velocity,
    north_velocity,
    depth,
    land_mask,
    wet_counts,
    loading_prev,
    tide_amp,
    tide_phase,
    legendre,
    love_factor,
):
    lon_dev, lat_dev = sea_level.shape
    wave_dev, degrees = legendre.shape[:2]
    lon_count = lax.axis_size("lon")
    lat_count = lax.axis_size("lat")
    total_cols = lon_dev * lon_count
    total_rows = lat_dev * lat_count
    bits = lon_count.bit_length() - 1
    lat_bits = lat_count.bit_length() - 1
    assert lon_count == 1 << bits and lat_count == 1 << lat_bits
    gens = [1] + [(1 << b) ^ 1 for b in (1, *range(bits - 1, 1, -1))][: bits - 1]
    vmem = pl.BlockSpec(memory_space=pltpu.VMEM)
    hbm = pl.BlockSpec(memory_space=pltpu.HBM)

    strip = shaped(6, MARGIN, LANES)

    def stay_put(cells):
        return pltpu.with_memory_space_constraint(cells, pltpu.HBM)

    fields = tuple(
        map(stay_put, (sea_level, east_velocity, north_velocity, depth, land_mask, loading_prev))
    )
    near, away = call(
        strip_kernel,
        [shaped(6 + lon_dev // MARGIN, MARGIN, LANES), strip],
        in_specs=[hbm] * 6,
        scratch=[
            pltpu.VMEM((lon_dev, lat_dev), jnp.int32),
            pltpu.SemaphoreType.DMA((2, 6)),
        ],
    )(*fields)
    own, *strips = call(
        pack_kernel,
        [shaped(6, lon_dev, lat_dev)] + [strip] * (1 if lat_count == 2 else 2),
        in_specs=[hbm] * 6,
        scratch=[
            pltpu.VMEM((lon_dev, lat_dev), jnp.int32),
            pltpu.SemaphoreType.DMA((6,)),
            pltpu.SemaphoreType.DMA,
        ],
    )(*fields)

    def stay(b):
        return b

    def nearby(b):
        return b ^ 1

    def beyond(b):
        return (b + 1 if b & 1 else b - 1) % lon_count

    def shift(cells, lat_step, move):
        pairs = []
        for a in range(lat_count):
            target = a ^ 1 if lat_step is None else a + lat_step
            if 0 <= target < lat_count:
                for b in range(lon_count):
                    pairs.append((a * lon_count + b, target * lon_count + move(b)))
        return lax.ppermute(cells, ("lat", "lon"), pairs)

    away = shift(away, 0, beyond)
    near = shift(near, 0, nearby)

    *strips, wet_pair = call(
        join_kernel,
        [shaped(12, MARGIN, LANES)] * len(strips)
        + [shaped(2 * lon_dev, lat_dev, dtype=bf16)],
    )(own, near, away, *strips)
    if lat_count == 2:
        facing = [shift(strips[0], None, stay)]
    else:
        facing = [shift(strips[1], -1, stay), shift(strips[0], 1, stay)]
    chunk = 2 * wave_dev
    lines = chunk * lon_count
    half = lines // 2
    wide = lon_dev + 2 * MARGIN
    forward, inverse, forcing, latitude, love, counts = call(
        functools.partial(
            table_kernel, (lon_dev, lat_dev, total_cols, total_rows, wave_dev, tuple(gens))
        ),
        [
            shaped(lines, 2 * lon_dev, dtype=bf16),
            shaped(2 * lon_dev, lines, dtype=bf16),
            shaped(SUBSTEPS, wide, 2 * lat_dev),
            shaped(3, 8, 2 * lat_dev),
            shaped(1, degrees),
            shaped(*wet_counts.shape, dtype=jnp.int32),
        ],
        in_specs=[hbm] * 4,
        scratch=[
            pltpu.VMEM((1, len(frequencies)), f32),
            pltpu.VMEM((1, len(frequencies)), f32),
            pltpu.VMEM((2, lon_count, lon_dev), f32),
            pltpu.SemaphoreType.DMA((4,)),
        ],
    )(
        stay_put(tide_amp[None]),
        stay_put(tide_phase[None]),
        stay_put(love_factor[None]),
        stay_put(wet_counts),
    )

    def swap(cells, gen):
        return lax.ppermute(cells, "lon", [(i, i ^ gen) for i in range(lon_count)])

    wet_far = swap(wet_pair, gens[1])

    held, send, wet_sum, state, static = call(
        functools.partial(step_kernel, lat_count),
        [
            shaped(2 * lon_dev, 2 * lat_dev, dtype=bf16),
            shaped(half + 8, lat_dev),
            shaped(8, lat_dev),
        ]
        + [pltpu.VMEM((3, wide, 2 * lat_dev), f32)] * 2,
        in_specs=[vmem] * (6 + len(facing)),
    )(own, near, away, *facing, forcing, latitude, forward)

    recv = swap(send, gens[0])
    keep = call(keep_kernel, shaped(half, lat_dev))(forward, held)
    wet_keep, wet_send = call(
        functools.partial(mask_kernel, (lon_dev, total_cols, wave_dev, tuple(gens))),
        [shaped(half // 4, lat_dev)] * 2,
    )(wet_pair, wet_far)
    wet_recv = swap(wet_send, gens[2])
    level = wet_sum + recv[half:]
    joined = lat_count == 2
    part = half // 2
    send = jnp.concatenate([keep[part:] + recv[part:half], level], axis=0)
    keep = keep[:part] + recv[:part]
    recv = swap(send, gens[1])
    arrived = recv[part:]
    if joined:
        arrived = arrived + shift(level, None, nearby)
        arrived = arrived + shift(level, None, lambda b: b ^ gens[1])
    level = level + arrived
    for place, gen in enumerate(gens[2:]):
        part = keep.shape[0] // 2
        sends = [keep[part:] + recv[part : 2 * part]]
        keep = keep[:part] + recv[:part]
        if place > 0:
            sends.append(wet_keep[part:] + wet_recv[part : 2 * part])
            wet_keep = wet_keep[:part] + wet_recv[:part]
        recv = swap(jnp.concatenate([*sends, level], axis=0), gen)
        if place > 0:
            wet_recv = recv[part : 2 * part]
            level = level + recv[2 * part :]
        else:
            level = level + recv[part:]
    if not joined:
        for b in range(lat_bits):
            level = level + lax.ppermute(
                level, "lat", [(i, i ^ (1 << b)) for i in range(lat_count)]
            )

    parts = 2
    waves = wave_dev // parts
    tables = []
    for piece in range(parts):
        tables.append(
            call(
                functools.partial(fetch_kernel, piece * waves),
                [
                    pltpu.VMEM((waves, degrees, lat_dev), bf16),
                    pltpu.VMEM((waves, lat_dev, degrees), bf16),
                ],
                in_specs=[hbm],
                scratch=[pltpu.SemaphoreType.DMA((4,))],
            )(stay_put(legendre))
        )
    turned = [table[1] for table in tables]
    tables = [table[0] for table in tables]
    pieces = ((0, wave_dev - wave_dev // 4), (wave_dev - wave_dev // 4, wave_dev // 4))
    sums = []
    for first, waves in pieces:
        mine, moving = call(
            functools.partial(analysis_kernel, (first, waves)),
            [shaped(2 * waves, degrees), shaped(2 * waves, degrees, dtype=bf16)],
            in_specs=[vmem] * 7,
        )(keep, recv, wet_keep, level, counts, *turned)
        for b in range(lat_bits):
            other = lax.ppermute(moving, "lat", [(i, i ^ (1 << b)) for i in range(lat_count)])
            if b < lat_bits - 1:
                mine = mine + other.astype(f32)
                moving = mine.astype(bf16)
        sums.append((mine, other))
    spectra = ()
    for piece, (first, waves) in enumerate(pieces):
        last = piece == len(pieces) - 1
        spectra = (
            call(
                functools.partial(synthesis_kernel, (first, waves, wave_dev)),
                shaped(2 * (first + waves), lat_dev, dtype=bf16 if last else f32),
                in_specs=[vmem] * (5 + len(spectra)),
            )(*sums[piece], love, *tables, *spectra),
        )
    near = spectra[0]
    for gen in gens[:0:-1]:
        near = jnp.concatenate([near, swap(near, gen)], axis=0)
    far = swap(near, gens[0])
    started = call(inverse_near_kernel, shaped(2 * lon_dev, lat_dev))(inverse, near)
    loading_new = call(inverse_far_kernel, shaped(lon_dev, lat_dev))(inverse, started, far)
    height, east_new, north_new = call(finish_kernel, [shaped(lon_dev, lat_dev)] * 3)(
        state, static, forcing, latitude
    )
    return (height, east_new, north_new, loading_new)


def solution(mesh):
    tile = P("lon", "lat")
    return jax.shard_map(
        shards,
        mesh=mesh,
        in_specs=(tile,) * 5 + (P(), tile, P(), P(), P("lon", None, "lat"), P()),
        out_specs=(tile,) * 4,
        check_vma=False,
    )
```
